128 devices in a mesh: dp: 4 (over z), ctx: 16 (over y, x_lo, core), tp: 2 (over x_hi).
Axes of the slice: x: 4 (x_hi: 2, x_lo: 2; x = x_hi * 2 + x_lo), y: 4, z: 4, core: 2. Of those that a mesh axis runs over, the one named last changes fastest.
Arguments:
- projected: bfloat16 [4, 2048, 3, 8192], P('dp', 'ctx', None, 'tp'), may hold values from -6 to 6
- upstream: bfloat16 [4, 2048, 8192], P('dp', 'ctx', 'tp'), may hold values from -6 to 6
- short_weight: float32 [3, 3, 8192], P(None, None, 'tp'), may hold values from -3.5 to 3.5
- skip_gain: float32 [8192], P('tp'), may hold values from 0.5 to 2
- residues: float32 [512, 16], replicated, may hold values from -2.5 to 2.5
- rates: float32 [512, 16], replicated, may hold values from 0.00024414062 to 0.05
Outputs:
- mixed: bfloat16 [4, 2048, 8192], P('dp', 'ctx', 'tp')
- grad_projected: bfloat16 [4, 2048, 3, 8192], P('dp', 'ctx', None, 'tp')
- grad_short: float32 [3, 3, 8192], P(None, None, 'tp')
- grad_skip: float32 [8192], P('tp')
- grad_residues: float32 [512, 16], replicated
- grad_log_rates: float32 [512, 16], replicated
The draws below stay inside these ranges and needn't reach their ends.
All inputs are finite; a program needn't handle non-finite values.
Results may differ from the reference program's by a relative error of at most 0.007.
Values may be sent and summed in bfloat16 or wider, within the bound.
A program may use at most 192 MiB of HBM per device.

```python
import math
import jax
import jax.numpy as jnp
from jax import lax

C = 8192
GROUP = 16
KSHORT = 3
ORDER = 16
BATCH = 4
LENGTH = 2048
GROUPS = 512


def levels(rng, dims, shards, smallest, largest):
    gain = 1.0
    for dim, blocks in shards:
        heights = jax.random.uniform(jax.random.fold_in(jax.random.fold_in(rng, 6), dim), (blocks,), jnp.float32, smallest / len(shards), largest / len(shards))
        gain = gain * jnp.repeat(jnp.exp(heights), dims[dim] // blocks).reshape((-1,) + (1,) * (len(dims) - 1 - dim))
    return gain


def bell_draw(stream_key, dims, spread, limit, split=(), kind=jnp.bfloat16):
    drawn = spread * jax.random.normal(stream_key, dims, jnp.float32)
    if split:
        drawn = drawn * levels(stream_key, dims, split, -0.22, 0.18)
    return jnp.clip(drawn, -limit, limit).astype(kind)


def setup_inputs(seed: int = 0) -> dict:
    splits = jax.random.split(jax.random.key(seed), 7)
    projected = bell_draw(splits[0], (BATCH, LENGTH, 3, C), 1.0, 6.0, ((0, 4), (1, 16), (3, 2)))
    upstream = bell_draw(splits[1], (BATCH, LENGTH, C), 1.0, 6.0, ((0, 4), (1, 16), (2, 2)))
    short_weight = bell_draw(splits[2], (3, KSHORT, C), KSHORT ** -0.5, 3.5, ((2, 2),), jnp.float32)
    skip_gain = jnp.clip(jnp.exp(math.log(2.0) - 1.3862944 * jax.random.uniform(splits[3], (C,), jnp.float32) ** levels(splits[3], (C,), ((0, 2),), -0.2, 0.2)), 0.5, 2.0)
    residues = bell_draw(splits[4], (GROUPS, ORDER), 0.35, 2.5, (), jnp.float32)
    rates = jnp.clip(jnp.exp(jax.random.uniform(splits[5], (GROUPS, ORDER), jnp.float32, math.log(0.00024414062), math.log(0.05))), 0.00024414062, 0.05)
    return {"projected": projected, "upstream": upstream, "short_weight": short_weight, "skip_gain": skip_gain, "residues": residues, "rates": rates}


PRECISE = lax.Precision.HIGHEST

def filter_taps(residues, rates, length):
    positions = jnp.arange(length, dtype=jnp.float32)
    decays = jnp.exp(-(rates[None, :, :] * positions[:, None, None]))
    taps_out = lax.optimization_barrier(jnp.sum(decays * (residues * jnp.sqrt(rates))[None, :, :], axis=2))
    return (taps_out, decays, positions)

def one_slab(slab_pair, short_weight, skip_gain, filter_freq):
    projected, upstream = slab_pair
    length = projected.shape[0]
    tap_count = short_weight.shape[1]
    padded = jnp.pad(projected.astype(jnp.float32), ((tap_count - 1, 0), (0, 0), (0, 0)))
    features = jnp.zeros(projected.shape, jnp.float32)
    for offset in range(tap_count):
        start_row = tap_count - 1 - offset
        features = features + padded[start_row:start_row + length] * short_weight[:, offset, :]
    query_part = features[:, 0]
    key_part = features[:, 1]
    value_part = features[:, 2]
    gated = (key_part * value_part).astype(jnp.bfloat16)
    gated_wide = gated.astype(jnp.float32)
    upstream_wide = upstream.astype(jnp.float32)
    grad_sum = upstream_wide * query_part
    grad_conv = grad_sum.astype(jnp.bfloat16)
    full_size = 2 * length
    gated_freq = jnp.fft.rfft(gated_wide, n=full_size, axis=0)
    grad_freq = jnp.fft.rfft(grad_conv.astype(jnp.float32), n=full_size, axis=0)
    channel_freq = jnp.repeat(filter_freq, GROUP, axis=1)
    convolved = jnp.fft.irfft(channel_freq * gated_freq, n=full_size, axis=0)[:length].astype(jnp.bfloat16)
    correlated = jnp.fft.irfft(jnp.conj(channel_freq) * grad_freq, n=full_size, axis=0)[:length].astype(jnp.bfloat16)
    cross_freq = lax.optimization_barrier(jnp.sum((jnp.conj(gated_freq) * grad_freq).reshape(length + 1, -1, GROUP), axis=2))
    filter_grad = jnp.fft.irfft(cross_freq, n=full_size, axis=0)[:length]
    mixture = convolved.astype(jnp.float32) + skip_gain * gated_wide
    mixed_out = (query_part * mixture).astype(jnp.bfloat16)
    grad_query = upstream_wide * mixture
    grad_gate = correlated.astype(jnp.float32) + skip_gain * grad_sum
    grad_rows = jnp.stack([grad_query, grad_gate * value_part, grad_gate * key_part], axis=1)
    extended = jnp.pad(grad_rows, ((0, tap_count - 1), (0, 0), (0, 0)))
    grad_input = jnp.zeros(grad_rows.shape, jnp.float32)
    short_terms = []
    for offset in range(tap_count):
        grad_input = grad_input + extended[offset:offset + length] * short_weight[:, offset, :]
        start_row = tap_count - 1 - offset
        short_terms.append(lax.optimization_barrier(jnp.sum(grad_rows * padded[start_row:start_row + length], axis=0)))
    grad_short = jnp.stack(short_terms, axis=1)
    grad_skip = lax.optimization_barrier(jnp.sum(grad_sum * gated_wide, axis=0))
    return (mixed_out, grad_input.astype(jnp.bfloat16), grad_short, grad_skip, filter_grad)

def reference(projected, upstream, short_weight, skip_gain, residues, rates):
    length = projected.shape[1]
    taps_out, decays, positions = filter_taps(residues, rates, length)
    filter_freq = jnp.fft.rfft(taps_out, n=2 * length, axis=0)

    def per_slab(slab_pair):
        return one_slab(slab_pair, short_weight, skip_gain, filter_freq)
    mixed, grad_projected, grad_short, grad_skip, filter_grad = lax.map(per_slab, (projected, upstream))
    norm_scale = 1.0 / math.sqrt(BATCH * LENGTH)
    grad_total = lax.optimization_barrier(jnp.sum(filter_grad, axis=0))
    sum_plain = jnp.einsum('sg,sgn->gn', grad_total, decays, precision=PRECISE)
    sum_weighted = jnp.einsum('sg,sgn->gn', grad_total * positions[:, None], decays, precision=PRECISE)
    rate_root = jnp.sqrt(rates)
    grad_residues = rate_root * sum_plain * norm_scale
    grad_log_rates = residues * (0.5 * rate_root * sum_plain - rates * rate_root * sum_weighted) * norm_scale
    return (mixed, grad_projected, lax.optimization_barrier(jnp.sum(grad_short, axis=0)) * norm_scale, lax.optimization_barrier(jnp.sum(grad_skip, axis=0)) * norm_scale, grad_residues, grad_log_rates)
```

```python
import functools
import math

import jax
import jax.numpy as jnp
from jax import lax
from jax.experimental import pallas as pl
from jax.experimental.pallas import tpu as pltpu
from jax.sharding import PartitionSpec as P

GROUP = 16
LANES = 128
PER_BLOCK = LANES // GROUP
PRECISE = lax.Precision.HIGHEST
MESH = pl.DeviceIdType.MESH
ROWS = 16


def shifted(value, axis, steps):
    count = lax.axis_size(axis)
    leading, last = (max(0, -steps), min(count, count - steps))
    return lax.ppermute(value, axis, [(source, source + steps) for source in range(leading, last)])


def iota(shape, axis):
    return lax.broadcasted_iota(jnp.int32, shape, axis)


def halves(value):
    high = value.astype(jnp.bfloat16)
    return high, (value - high.astype(jnp.float32)).astype(jnp.bfloat16)


def dot(left, right, dims=((1,), (0,)), precision=None):
    return lax.dot_general(
        left, right, (dims, ((), ())), precision=precision, preferred_element_type=jnp.float32
    )


def flip_matrix(size):
    return (iota((size, size), 0) + iota((size, size), 1) == size - 1).astype(jnp.bfloat16)


def decay_table(rate_row, size):
    ages = (size - 1 - iota((size, LANES), 0)).astype(jnp.float32)
    table = jnp.exp(-(rate_row * ages))
    return table, ages * table


def to_row(value):
    rows = iota((LANES, LANES), 0)
    cols = iota((LANES, LANES), 1)
    same = (rows // GROUP == cols // GROUP).astype(jnp.float32)
    summed = dot(value, same, precision=PRECISE)
    pick = iota(value.shape, 0) == iota(value.shape, 1) % GROUP
    return jnp.sum(jnp.where(pick, summed, 0.0), axis=0, keepdims=True)


def to_wide(rate_row):
    rows = iota((LANES, LANES), 0)
    cols = iota((LANES, LANES), 1)
    same = (rows // GROUP == cols // GROUP).astype(jnp.float32)
    pick = iota((GROUP, LANES), 0) == iota((GROUP, LANES), 1) % GROUP
    return dot(jnp.where(pick, jnp.broadcast_to(rate_row, (GROUP, LANES)), 0.0), same, precision=PRECISE)


def delayed(value, halo):
    row = iota(value.shape, 0)
    one = jnp.where(row == 0, halo[1:2], pltpu.roll(value, 1, 0))
    two = jnp.where(row == 0, halo[0:1], jnp.where(row == 1, halo[1:2], pltpu.roll(value, 2, 0)))
    return one, two


def features_of(proj_ref, halo_ref, weight_ref, lanes):
    outs = []
    taps = []
    for part in range(3):
        now = proj_ref[part, :, lanes].astype(jnp.float32)
        halo = halo_ref[part, :, lanes].astype(jnp.float32)
        one, two = delayed(now, halo)
        weight = weight_ref[part, :, lanes]
        outs.append(now * weight[0:1] + one * weight[1:2] + two * weight[2:3])
        taps.append((now, one, two))
    return outs, taps


def gather_kernel(blocks, proj_ref, halo_ref, up_ref, weight_ref, rate_ref, x_ref, state_ref, slope_ref):
    size = proj_ref.shape[1]
    for block in range(blocks):
        lanes = pl.ds(block * LANES, LANES)
        (query, key, value), _ = features_of(proj_ref, halo_ref, weight_ref, lanes)
        gated = (key * value).astype(jnp.bfloat16)
        grad = (up_ref[:, lanes].astype(jnp.float32) * query).astype(jnp.bfloat16)
        turned = dot(flip_matrix(size), grad).astype(jnp.bfloat16)
        both = jnp.concatenate([gated, turned], axis=1)
        x_ref[block] = both
        table, slope = decay_table(rate_ref[block], size)
        keep = iota((LANES, 2 * LANES), 0) // GROUP == iota((LANES, 2 * LANES), 1) % LANES // GROUP
        for source, target in ((table, state_ref), (slope, slope_ref)):
            high, low = halves(source)
            full = dot(high, both, ((0,), (0,))) + dot(low, both, ((0,), (0,)))
            full = jnp.where(keep, full, 0.0)
            target[block] = jnp.sum(full.reshape(PER_BLOCK, GROUP, 2 * LANES), axis=0)


def inner_kernel(blocks, x_ref, rate_ref, gain_ref, y_ref, mode_ref):
    size = x_ref.shape[1]
    row = iota((size, LANES), 0)
    col = iota((size, LANES), 1)
    lane_group = col // GROUP
    wide_group = iota((size, 2 * LANES), 1) % LANES // GROUP
    small_keep = iota((PER_BLOCK, LANES), 0) == iota((PER_BLOCK, LANES), 1) // GROUP
    for block in range(blocks):
        both = x_ref[block]
        gated = both[:, :LANES]
        turned = both[:, LANES:]
        table, slope = decay_table(rate_ref[block], size)
        spread = jnp.where(small_keep, jnp.broadcast_to(gain_ref[block], (PER_BLOCK, LANES)), 0.0)
        taps = dot(spread, table, ((1,), (1,)), PRECISE)
        total = jnp.zeros((size, 2 * LANES), jnp.float32)
        sums = []
        for group in range(PER_BLOCK):
            line = jnp.broadcast_to(taps[group : group + 1], (size, LANES))
            band = pltpu.roll(line, 1, 1, stride=1, stride_axis=0)
            band = jnp.where(col <= row, band, 0.0).astype(jnp.bfloat16)
            total = jnp.where(wide_group == group, dot(band, both), total)
            chosen = jnp.where(lane_group == group, turned, jnp.zeros_like(turned))
            cross = dot(chosen, gated, ((1,), (1,)))
            cross = pltpu.roll(cross, 0, 1, stride=1, stride_axis=0)
            sums.append(jnp.sum(jnp.where(col >= row, cross, 0.0), axis=0, keepdims=True))
        y_ref[block] = total
        lags = jnp.concatenate(sums, axis=0)
        outs = []
        for source in (table, slope):
            spread = dot(lags, source, precision=PRECISE)
            outs.append(jnp.sum(jnp.where(small_keep, spread, 0.0), axis=0, keepdims=True))
        mode_ref[block] = jnp.concatenate(outs + [jnp.zeros((6, LANES), jnp.float32)], axis=0)


def scan_kernel(size, recv_ref, rate_ref, carry_ref, extra_ref):
    count = recv_ref.shape[0]
    for block in range(recv_ref.shape[1]):
        rate_row = rate_ref[block]
        decay = jnp.exp(-(to_wide(rate_row) * float(size)))
        held = jnp.zeros((GROUP, LANES), jnp.float32)
        aged = held
        plain = held
        weighted = held
        for step in range(count):
            begin = recv_ref[step, block, :, :LANES]
            other = recv_ref[step, block, :, LANES:]
            carry_ref[step, block, :, :LANES] = held
            plain = plain + other * held
            weighted = weighted + other * aged
            aged = decay * (aged + held)
            held = decay * held + begin
        held = jnp.zeros((GROUP, LANES), jnp.float32)
        for step in reversed(range(count)):
            carry_ref[step, block, :, LANES:] = held
            held = recv_ref[step, block, :, LANES:] + decay * held
        once = jnp.exp(-rate_row)
        extra_ref[block] = jnp.concatenate(
            [
                jnp.zeros((10, LANES), jnp.float32),
                once * to_row(plain),
                once * to_row(plain + float(size) * weighted),
                jnp.zeros((4, LANES), jnp.float32),
            ],
            axis=0,
        )


def outer_kernel(
    blocks, norm, proj_ref, halo_ref, up_ref, weight_ref, skip_ref, rate_ref, gain_ref, y_ref,
    carry_ref, slope_ref, mode_ref, mixed_ref, grad_ref, first_ref, last_ref, part_ref,
):
    size = proj_ref.shape[1]
    row = iota((size, LANES), 0)
    keep = iota((LANES, 2 * LANES), 0) // GROUP == iota((LANES, 2 * LANES), 1) % LANES // GROUP
    ages = (iota((size, LANES), 0) + 1).astype(jnp.float32)
    for block in range(blocks):
        lanes = pl.ds(block * LANES, LANES)
        (query, key, value), taps = features_of(proj_ref, halo_ref, weight_ref, lanes)
        gated = (key * value).astype(jnp.bfloat16).astype(jnp.float32)
        rate_row = rate_ref[block]
        coef = gain_ref[block] * jnp.exp(-(rate_row * ages))
        coef_high, coef_low = halves(coef)
        carry = carry_ref[block]
        spread = jnp.where(keep, jnp.concatenate([carry] * PER_BLOCK, axis=0), 0.0)
        high, low = halves(spread)
        whole = y_ref[block] + (dot(coef_high, high) + (dot(coef_high, low) + dot(coef_low, high)))
        narrow = whole.astype(jnp.bfloat16)
        convolved = narrow[:, :LANES].astype(jnp.float32)
        correlated = dot(flip_matrix(size), narrow[:, LANES:])
        upstream = up_ref[:, lanes].astype(jnp.float32)
        skip = skip_ref[:, lanes]
        grad_sum = upstream * query
        mixture = convolved + skip * gated
        mixed_ref[:, lanes] = (query * mixture).astype(jnp.bfloat16)
        grad_gate = correlated + skip * grad_sum
        lines = []
        for part, grads in enumerate((upstream * mixture, grad_gate * value, grad_gate * key)):
            weight = weight_ref[part, :, lanes]
            ahead = jnp.where(row < size - 1, pltpu.roll(grads, size - 1, 0), 0.0)
            further = jnp.where(row < size - 2, pltpu.roll(grads, size - 2, 0), 0.0)
            result = grads * weight[0:1] + ahead * weight[1:2] + further * weight[2:3]
            grad_ref[part, :, lanes] = result.astype(jnp.bfloat16)
            first_ref[part, :, lanes] = grads[:8]
            last_ref[part, :, lanes] = result[size - 8 :]
            for tap in taps[part]:
                lines.append(jnp.sum(grads * tap, axis=0, keepdims=True) * norm)
        lines.append(jnp.sum(grad_sum * gated, axis=0, keepdims=True) * norm)
        slopes = slope_ref[block]
        between = slopes[:, LANES:] * carry[:, :LANES] + slopes[:, :LANES] * carry[:, LANES:]
        modes = mode_ref[block]
        lines.append(modes[0:1])
        lines.append(modes[1:2] + jnp.exp(-rate_row) * to_row(between))
        lines.append(jnp.zeros((4, LANES), jnp.float32))
        part_ref[block] = jnp.concatenate(lines, axis=0)


def mend_kernel(grad_ref, last_ref, after_ref, weight_ref, out_ref):
    for part in range(3):
        tile = grad_ref[part]
        last = last_ref[part]
        after = after_ref[part]
        weight = weight_ref[part]
        late = last[6:7] + after[0:1] * weight[2:3]
        final = last[7:8] + after[0:1] * weight[1:2] + after[1:2] * weight[2:3]
        row = iota(tile.shape, 0)
        wide = jnp.where(row == 14, late, jnp.where(row == 15, final, tile.astype(jnp.float32)))
        out_ref[part] = wide.astype(jnp.bfloat16)


def reduce_kernel(
    counts, part_ref, extra_ref, out_ref, near_ref, sum_ref, far_ref, done_ref,
    send_one, recv_one, send_two, recv_two, send_three, recv_three,
):
    dp_count, ctx_count, tp_count = counts
    dp, ctx, tp = lax.axis_index("dp"), lax.axis_index("ctx"), lax.axis_index("tp")
    others = [(a, b) for b in range(tp_count) for a in range(dp_count) if (a, b) != (0, 0)]

    def ring(step):
        return {"ctx": lax.rem(ctx + step, ctx_count)}

    def cross(pair):
        return {"dp": lax.rem(dp + pair[0], dp_count), "tp": lax.rem(tp + pair[1], tp_count)}

    barrier = pltpu.get_barrier_semaphore()
    for step in range(1, ctx_count):
        pl.semaphore_signal(barrier, inc=1, device_id=ring(step), device_id_type=MESH)
    for pair in others:
        pl.semaphore_signal(barrier, inc=1, device_id=cross(pair), device_id_type=MESH)
    pl.semaphore_wait(barrier, ctx_count - 1 + len(others))

    first = []
    for step in range(1, ctx_count):
        first.append(
            pltpu.make_async_remote_copy(
                part_ref.at[lax.rem(ctx + step, ctx_count)], near_ref.at[step],
                send_one.at[step], recv_one.at[step], device_id=ring(step), device_id_type=MESH,
            )
        )
        first[-1].start()
    total = part_ref[ctx] + extra_ref[...]
    for step in range(1, ctx_count):
        first[step - 1].wait_recv()
        total = total + near_ref[step]
    sum_ref[...] = total

    second = []
    for index, pair in enumerate(others):
        second.append(
            pltpu.make_async_remote_copy(
                sum_ref, far_ref.at[index], send_two.at[index], recv_two.at[index],
                device_id=cross(pair), device_id_type=MESH,
            )
        )
        second[-1].start()
    foreign = jnp.zeros_like(total)
    for index, pair in enumerate(others):
        second[index].wait_recv()
        if pair[1] == 0:
            total = total + far_ref[index]
        else:
            foreign = foreign + far_ref[index]
    moved = pltpu.roll(foreign, 2, 1)
    row = iota(total.shape, 1)
    total = jnp.where((row == 12) | (row == 13), moved, total)
    done_ref[...] = total

    third = []
    for step in range(1, ctx_count):
        third.append(
            pltpu.make_async_remote_copy(
                done_ref, out_ref.at[ctx], send_three.at[step], recv_three.at[step],
                device_id=ring(step), device_id_type=MESH,
            )
        )
        third[-1].start()
    out_ref[ctx] = total
    for copy in third:
        copy.wait_recv()
    for copy in first + second + third:
        copy.wait_send()


def local(projected, upstream, short_weight, skip_gain, residues, rates):
    size = projected.shape[1]
    width = projected.shape[3]
    dp_count, ctx_count, tp_count = (lax.axis_size(name) for name in ("dp", "ctx", "tp"))
    block_count = width // LANES
    own_blocks = block_count // ctx_count
    group_count = width // GROUP
    blocks = math.gcd(block_count, 4)
    norm = 1.0 / math.sqrt(dp_count * ctx_count * size)

    proj = projected[0].transpose(1, 0, 2)
    up = upstream[0]
    before = shifted(proj[:, size - 2 :], "ctx", 1)
    tp = lax.axis_index("tp")
    ctx = lax.axis_index("ctx")
    my_rates = lax.dynamic_slice_in_dim(rates, tp * group_count, group_count, 0)
    my_residues = lax.dynamic_slice_in_dim(residues, tp * group_count, group_count, 0)
    rate_rows = my_rates.reshape(block_count, 1, LANES)
    gain_rows = (my_residues * jnp.sqrt(my_rates)).reshape(block_count, 1, LANES)
    own_rates = lax.dynamic_slice_in_dim(rate_rows, ctx * own_blocks, own_blocks, 0)
    skip_row = skip_gain.reshape(1, width)

    grid = (block_count // blocks,)
    step_width = blocks * LANES
    wide3 = pl.BlockSpec((3, size, step_width), lambda i: (0, 0, i))
    halo3 = pl.BlockSpec((3, 2, step_width), lambda i: (0, 0, i))
    tile3 = pl.BlockSpec((3, 8, step_width), lambda i: (0, 0, i))
    taps3 = pl.BlockSpec((3, 3, step_width), lambda i: (0, 0, i))
    flat = pl.BlockSpec((size, step_width), lambda i: (0, i))
    line = pl.BlockSpec((1, step_width), lambda i: (0, i))

    def stacked(rows, cols):
        return pl.BlockSpec((blocks, rows, cols), lambda i: (i, 0, 0))

    def array(*shape, kind=jnp.float32):
        return jax.ShapeDtypeStruct(shape, kind)

    row_spec = stacked(1, LANES)
    params = pltpu.CompilerParams(dimension_semantics=("arbitrary",))

    x, states, slopes = pl.pallas_call(
        functools.partial(gather_kernel, blocks),
        grid=grid,
        in_specs=[wide3, halo3, flat, taps3, row_spec],
        out_specs=[stacked(size, 2 * LANES), stacked(GROUP, 2 * LANES), stacked(GROUP, 2 * LANES)],
        out_shape=[
            array(block_count, size, 2 * LANES, kind=jnp.bfloat16),
            array(block_count, GROUP, 2 * LANES),
            array(block_count, GROUP, 2 * LANES),
        ],
        compiler_params=params,
        name="states",
    )(proj, before, up, short_weight, rate_rows)

    received = lax.all_to_all(
        states.reshape(ctx_count, own_blocks, GROUP, 2 * LANES), "ctx", 0, 0, tiled=True
    )

    y, modes = pl.pallas_call(
        functools.partial(inner_kernel, blocks),
        grid=grid,
        in_specs=[stacked(size, 2 * LANES), row_spec, row_spec],
        out_specs=[stacked(size, 2 * LANES), stacked(8, LANES)],
        out_shape=[array(block_count, size, 2 * LANES), array(block_count, 8, LANES)],
        compiler_params=params,
        cost_estimate=pl.CostEstimate(
            flops=4 * block_count * 8 * size * size * LANES * 3,
            bytes_accessed=block_count * size * 256 * 6,
            transcendentals=block_count * size * LANES,
        ),
        name="inner",
    )(x, rate_rows, gain_rows)

    carry, extra = pl.pallas_call(
        functools.partial(scan_kernel, size),
        out_shape=[
            array(ctx_count, own_blocks, GROUP, 2 * LANES),
            array(own_blocks, ROWS, LANES),
        ],
        name="scan",
    )(received, own_rates)
    carry = lax.all_to_all(carry, "ctx", 0, 0, tiled=True).reshape(block_count, GROUP, 2 * LANES)

    mixed, grad, first, last, part = pl.pallas_call(
        functools.partial(outer_kernel, blocks, norm),
        grid=grid,
        in_specs=[
            wide3, halo3, flat, taps3, line, row_spec, row_spec, stacked(size, 2 * LANES),
            stacked(GROUP, 2 * LANES), stacked(GROUP, 2 * LANES), stacked(8, LANES),
        ],
        out_specs=[flat, wide3, tile3, tile3, stacked(ROWS, LANES)],
        out_shape=[
            array(size, width, kind=jnp.bfloat16),
            array(3, size, width, kind=jnp.bfloat16),
            array(3, 8, width),
            array(3, 8, width),
            array(block_count, ROWS, LANES),
        ],
        compiler_params=params,
        name="outer",
    )(proj, before, up, short_weight, skip_row, rate_rows, gain_rows, y, carry, slopes, modes)

    after = shifted(first[:, :2], "ctx", -1)

    others = dp_count * tp_count - 1
    summed = pl.pallas_call(
        functools.partial(reduce_kernel, (dp_count, ctx_count, tp_count)),
        in_specs=[pl.BlockSpec(memory_space=pltpu.VMEM)] * 2,
        out_specs=pl.BlockSpec(memory_space=pltpu.VMEM),
        out_shape=array(ctx_count, own_blocks, ROWS, LANES),
        scratch_shapes=[
            pltpu.VMEM((ctx_count, own_blocks, ROWS, LANES), jnp.float32),
            pltpu.VMEM((own_blocks, ROWS, LANES), jnp.float32),
            pltpu.VMEM((max(others, 1), own_blocks, ROWS, LANES), jnp.float32),
            pltpu.VMEM((own_blocks, ROWS, LANES), jnp.float32),
            pltpu.SemaphoreType.DMA((ctx_count,)),
            pltpu.SemaphoreType.DMA((ctx_count,)),
            pltpu.SemaphoreType.DMA((max(others, 1),)),
            pltpu.SemaphoreType.DMA((max(others, 1),)),
            pltpu.SemaphoreType.DMA((ctx_count,)),
            pltpu.SemaphoreType.DMA((ctx_count,)),
        ],
        compiler_params=pltpu.CompilerParams(collective_id=0, has_side_effects=True),
        name="reduce",
    )(part.reshape(ctx_count, own_blocks, ROWS, LANES), extra)

    mend_width = math.gcd(width, 1024)
    tail = pl.BlockSpec((3, 16, mend_width), lambda i: (0, size // 16 - 1, i))
    grad = pl.pallas_call(
        mend_kernel,
        grid=(width // mend_width,),
        in_specs=[
            tail,
            pl.BlockSpec((3, 8, mend_width), lambda i: (0, 0, i)),
            pl.BlockSpec((3, 2, mend_width), lambda i: (0, 0, i)),
            pl.BlockSpec((3, 3, mend_width), lambda i: (0, 0, i)),
        ],
        out_specs=tail,
        out_shape=array(3, size, width, kind=jnp.bfloat16),
        input_output_aliases={0: 0},
        compiler_params=params,
        name="mend",
    )(grad, last, after, short_weight)

    flat_sums = summed.reshape(block_count, ROWS, LANES)
    grad_short = flat_sums[:, :9].transpose(1, 0, 2).reshape(3, 3, width)
    grad_skip = flat_sums[:, 9].reshape(width)

    def both_halves(index):
        mine = flat_sums[:, 10 + index].reshape(1, group_count, GROUP)
        if tp_count == 1:
            return mine.reshape(group_count, GROUP)
        other = flat_sums[:, 12 + index].reshape(1, group_count, GROUP)
        low = jnp.where(tp == 0, mine, other)
        high = jnp.where(tp == 0, other, mine)
        return jnp.concatenate([low, high], axis=0).reshape(2 * group_count, GROUP)

    sum_plain = both_halves(0)
    sum_weighted = both_halves(1)
    root = jnp.sqrt(rates)
    grad_residues = root * sum_plain * norm
    grad_log_rates = residues * (0.5 * root * sum_plain - rates * root * sum_weighted) * norm
    return (
        mixed[None],
        grad.transpose(1, 0, 2)[None],
        grad_short,
        grad_skip,
        grad_residues,
        grad_log_rates,
    )


def solution(mesh):
    in_specs = (
        P("dp", "ctx", None, "tp"),
        P("dp", "ctx", "tp"),
        P(None, None, "tp"),
        P("tp"),
        P(),
        P(),
    )
    out_specs = (
        P("dp", "ctx", "tp"),
        P("dp", "ctx", None, "tp"),
        P(None, None, "tp"),
        P("tp"),
        P(),
        P(),
    )
    return jax.shard_map(local, mesh=mesh, in_specs=in_specs, out_specs=out_specs, check_vma=False)
```

```python
import functools
import math

import jax
import jax.numpy as jnp
from jax import lax
from jax.experimental import pallas as pl
from jax.experimental.pallas import tpu as pltpu
from jax.sharding import PartitionSpec as P

GROUP = 16
LANES = 128
PER_BLOCK = LANES // GROUP
PRECISE = lax.Precision.HIGHEST
MESH = pl.DeviceIdType.MESH
ROWS = 16
SUB = 32


def shifted(value, axis, steps):
    count = lax.axis_size(axis)
    leading, last = (max(0, -steps), min(count, count - steps))
    return lax.ppermute(value, axis, [(source, source + steps) for source in range(leading, last)])


def iota(shape, axis):
    return lax.broadcasted_iota(jnp.int32, shape, axis)


def halves(value):
    high = value.astype(jnp.bfloat16)
    return high, (value - high.astype(jnp.float32)).astype(jnp.bfloat16)


def dot(left, right, dims=((1,), (0,)), precision=None):
    return lax.dot_general(
        left, right, (dims, ((), ())), precision=precision, preferred_element_type=jnp.float32
    )


def flip_matrix(size):
    return (iota((size, size), 0) + iota((size, size), 1) == size - 1).astype(jnp.bfloat16)


def decay_table(rate_row, size):
    ages = (size - 1 - iota((size, LANES), 0)).astype(jnp.float32)
    table = jnp.exp(-(rate_row * ages))
    return table, ages * table


def to_row(value):
    rows = iota((LANES, LANES), 0)
    cols = iota((LANES, LANES), 1)
    same = (rows // GROUP == cols // GROUP).astype(jnp.float32)
    summed = dot(value, same, precision=PRECISE)
    pick = iota(value.shape, 0) == iota(value.shape, 1) % GROUP
    return jnp.sum(jnp.where(pick, summed, 0.0), axis=0, keepdims=True)


def to_wide(rate_row):
    rows = iota((LANES, LANES), 0)
    cols = iota((LANES, LANES), 1)
    same = (rows // GROUP == cols // GROUP).astype(jnp.float32)
    pick = iota((GROUP, LANES), 0) == iota((GROUP, LANES), 1) % GROUP
    return dot(jnp.where(pick, jnp.broadcast_to(rate_row, (GROUP, LANES)), 0.0), same, precision=PRECISE)


def delayed(value, halo):
    row = iota(value.shape, 0)
    one = jnp.where(row == 0, halo[1:2], pltpu.roll(value, 1, 0))
    two = jnp.where(row == 0, halo[0:1], jnp.where(row == 1, halo[1:2], pltpu.roll(value, 2, 0)))
    return one, two


def features_of(proj_ref, halo_ref, weight_ref, lanes):
    outs = []
    taps = []
    for part in range(3):
        now = proj_ref[part, :, lanes].astype(jnp.float32)
        halo = halo_ref[part, :, lanes].astype(jnp.float32)
        one, two = delayed(now, halo)
        weight = weight_ref[part, :, lanes]
        outs.append(now * weight[0:1] + one * weight[1:2] + two * weight[2:3])
        taps.append((now, one, two))
    return outs, taps


def gather_kernel(blocks, proj_ref, halo_ref, up_ref, weight_ref, rate_ref, x_ref, state_ref, slope_ref):
    size = proj_ref.shape[1]
    for block in range(blocks):
        lanes = pl.ds(block * LANES, LANES)
        (query, key, value), _ = features_of(proj_ref, halo_ref, weight_ref, lanes)
        gated = (key * value).astype(jnp.bfloat16)
        grad = (up_ref[:, lanes].astype(jnp.float32) * query).astype(jnp.bfloat16)
        turned = dot(flip_matrix(size), grad).astype(jnp.bfloat16)
        both = jnp.concatenate([gated, turned], axis=1)
        x_ref[block] = both
        table, slope = decay_table(rate_ref[block], size)
        keep = iota((LANES, 2 * LANES), 0) // GROUP == iota((LANES, 2 * LANES), 1) % LANES // GROUP
        for source, target in ((table, state_ref), (slope, slope_ref)):
            high, low = halves(source)
            full = dot(high, both, ((0,), (0,))) + dot(low, both, ((0,), (0,)))
            full = jnp.where(keep, full, 0.0)
            target[block] = jnp.sum(full.reshape(PER_BLOCK, GROUP, 2 * LANES), axis=0)


def inner_blocks(base, blocks, x_ref, rate_ref, gain_ref, y_ref, mode_ref):
    size = x_ref.shape[1]
    runs = size // SUB
    small_keep = iota((PER_BLOCK, LANES), 0) == iota((PER_BLOCK, LANES), 1) // GROUP
    lag_lane = iota((PER_BLOCK, LANES), 1)
    lag_seat = iota((PER_BLOCK, LANES), 0) % runs
    keep = (
        iota((PER_BLOCK * SUB, 2 * LANES), 0) // SUB
        == iota((PER_BLOCK * SUB, 2 * LANES), 1) % LANES // GROUP
    )
    causal = iota((SUB, size), 1) >= iota((SUB, size), 0)
    parity = iota((SUB, LANES), 1) // SUB % 2
    steps = iota((size, LANES), 0).astype(jnp.float32)
    every = range(blocks)
    tables = [decay_table(rate_ref[base + block], size) for block in every]
    taps = []
    for block in every:
        forward = jnp.exp(-(rate_ref[base + block] * steps))
        spread = jnp.where(small_keep, jnp.broadcast_to(gain_ref[base + block], (PER_BLOCK, LANES)), 0.0)
        taps.append(dot(spread, forward, ((1,), (1,)), PRECISE))
    chosen = []
    for block in every:
        picks = []
        for run in range(runs):
            tiled = jnp.concatenate([x_ref[base + block, run * SUB : (run + 1) * SUB]] * PER_BLOCK, axis=0)
            picks.append(jnp.where(keep, tiled, jnp.zeros_like(tiled)))
        chosen.append(picks)

    def stepped(value):
        parts = [value]
        for run in range(1, runs):
            blank = jnp.zeros((run * SUB, value.shape[1]), value.dtype)
            parts.append(jnp.concatenate([blank, value[: size - run * SUB]], axis=0))
        return jnp.concatenate(parts, axis=1)

    crosses = [
        dot(
            stepped(x_ref[base + block, :, LANES:]),
            jnp.concatenate([value[:, :LANES] for value in chosen[block]], axis=1),
            ((1,), (1,)),
        )
        for block in every
    ]
    lefts = []
    for block in every:
        bands = []
        for group in range(PER_BLOCK):
            line = jnp.broadcast_to(taps[block][group : group + 1], (SUB, size))
            line = pltpu.roll(line, 0, 1, stride=1, stride_axis=0)
            bands.append(jnp.where(causal, line, 0.0))
        lefts.append(jnp.concatenate(bands, axis=0).T.astype(jnp.bfloat16))
    for block in every:
        y_ref[base + block] = dot(stepped(lefts[block]), jnp.concatenate(chosen[block], axis=0))
    lags = []
    for block in every:
        packed = []
        for run in range(runs):
            lines = []
            for tile in range(2):
                part = crosses[block][run * SUB : (run + 1) * SUB, tile * LANES : (tile + 1) * LANES]
                two = []
                for odd in range(2):
                    moved = jnp.where(parity == odd, part, 0.0)
                    moved = pltpu.roll(moved, 0, 1, stride=1, stride_axis=0)
                    two.append(jnp.sum(moved, axis=0, keepdims=True))
                lines += [two[0], two[1], two[0], two[1]]
            packed.append(jnp.concatenate(lines, axis=0))
        total = jnp.zeros((PER_BLOCK, LANES), jnp.float32)
        for turn in range(runs):
            lag_run = (lag_seat + turn) % runs
            lines = packed[0]
            for run in range(1, runs):
                lines = jnp.where(lag_run == run, packed[run], lines)
            if turn:
                lines = pltpu.roll(lines, turn * SUB, 1)
            begin = lag_run * SUB
            inside = (lag_lane >= begin) & (lag_lane < begin + 2 * SUB - 1)
            total = total + jnp.where(inside, lines, 0.0)
        lags.append(total)
    spreads = [[dot(lags[block], source, precision=PRECISE) for source in tables[block]] for block in every]
    for block in every:
        outs = [
            jnp.sum(jnp.where(small_keep, spread, 0.0), axis=0, keepdims=True) for spread in spreads[block]
        ]
        mode_ref[base + block] = jnp.concatenate(outs + [jnp.zeros((6, LANES), jnp.float32)], axis=0)


def scan_states(size, ctx, count, recv_ref, rate_ref, carry_ref, extra_ref):
    slots = [lax.rem(ctx - step + count, count) for step in range(count)]
    for block in range(recv_ref.shape[1]):
        rate_row = rate_ref[block]
        decay = jnp.exp(-(to_wide(rate_row) * float(size)))
        held = jnp.zeros((GROUP, LANES), jnp.float32)
        aged = held
        plain = held
        weighted = held
        for step in range(count):
            begin = recv_ref[slots[step], block, :, :LANES]
            other = recv_ref[slots[step], block, :, LANES:]
            carry_ref[step, block, :, :LANES] = held
            plain = plain + other * held
            weighted = weighted + other * aged
            aged = decay * (aged + held)
            held = decay * held + begin
        held = jnp.zeros((GROUP, LANES), jnp.float32)
        for step in reversed(range(count)):
            carry_ref[step, block, :, LANES:] = held
            held = recv_ref[slots[step], block, :, LANES:] + decay * held
        once = jnp.exp(-rate_row)
        extra_ref[block] = jnp.concatenate(
            [
                jnp.zeros((10, LANES), jnp.float32),
                once * to_row(plain),
                once * to_row(plain + float(size) * weighted),
                jnp.zeros((4, LANES), jnp.float32),
            ],
            axis=0,
        )


def exchange_kernel(
    ctx_count, blocks, early, state_ref, x_ref, rate_ref, gain_ref, own_ref, y_ref, mode_ref, carry_ref,
    extra_ref, near_ref, back_ref, send_one, recv_one, send_two, recv_two,
):
    ctx = lax.axis_index("ctx")
    size = x_ref.shape[1]
    rounds = x_ref.shape[0] // blocks

    def peer(step):
        return lax.rem(ctx + step, ctx_count)

    def work(index, carry):
        inner_blocks(index * blocks, blocks, x_ref, rate_ref, gain_ref, y_ref, mode_ref)
        return carry

    barrier = pltpu.get_barrier_semaphore()
    for step in range(1, ctx_count):
        pl.semaphore_signal(barrier, inc=1, device_id={"ctx": peer(step)}, device_id_type=MESH)
    pl.semaphore_wait(barrier, ctx_count - 1)
    first = []
    for step in range(1, ctx_count):
        first.append(
            pltpu.make_async_remote_copy(
                state_ref.at[peer(step)], near_ref.at[step], send_one.at[step], recv_one.at[step],
                device_id={"ctx": peer(step)}, device_id_type=MESH,
            )
        )
        first[-1].start()
    near_ref[0] = state_ref[ctx]
    lax.fori_loop(0, early, work, 0)
    for copy in first:
        copy.wait_recv()
    scan_states(size, ctx, ctx_count, near_ref, own_ref, back_ref, extra_ref)
    second = []
    for step in range(1, ctx_count):
        second.append(
            pltpu.make_async_remote_copy(
                back_ref.at[peer(step)], carry_ref.at[ctx], send_two.at[step], recv_two.at[step],
                device_id={"ctx": peer(step)}, device_id_type=MESH,
            )
        )
        second[-1].start()
    carry_ref[ctx] = back_ref[ctx]
    lax.fori_loop(early, rounds, work, 0)
    for copy in second:
        copy.wait_recv()
    for copy in first + second:
        copy.wait_send()


def outer_kernel(
    blocks, norm, proj_ref, halo_ref, up_ref, weight_ref, skip_ref, rate_ref, gain_ref, y_ref,
    carry_ref, slope_ref, mode_ref, mixed_ref, grad_ref, first_ref, last_ref, part_ref,
):
    size = proj_ref.shape[1]
    row = iota((size, LANES), 0)
    keep = iota((LANES, 2 * LANES), 0) // GROUP == iota((LANES, 2 * LANES), 1) % LANES // GROUP
    ages = (iota((size, LANES), 0) + 1).astype(jnp.float32)
    for block in range(blocks):
        lanes = pl.ds(block * LANES, LANES)
        (query, key, value), taps = features_of(proj_ref, halo_ref, weight_ref, lanes)
        gated = (key * value).astype(jnp.bfloat16).astype(jnp.float32)
        rate_row = rate_ref[block]
        coef = gain_ref[block] * jnp.exp(-(rate_row * ages))
        coef_high, coef_low = halves(coef)
        carry = carry_ref[block]
        spread = jnp.where(keep, jnp.concatenate([carry] * PER_BLOCK, axis=0), 0.0)
        high, low = halves(spread)
        whole = y_ref[block] + (dot(coef_high, high) + (dot(coef_high, low) + dot(coef_low, high)))
        narrow = whole.astype(jnp.bfloat16)
        convolved = narrow[:, :LANES].astype(jnp.float32)
        correlated = dot(flip_matrix(size), narrow[:, LANES:])
        upstream = up_ref[:, lanes].astype(jnp.float32)
        skip = skip_ref[:, lanes]
        grad_sum = upstream * query
        mixture = convolved + skip * gated
        mixed_ref[:, lanes] = (query * mixture).astype(jnp.bfloat16)
        grad_gate = correlated + skip * grad_sum
        lines = []
        for part, grads in enumerate((upstream * mixture, grad_gate * value, grad_gate * key)):
            weight = weight_ref[part, :, lanes]
            ahead = jnp.where(row < size - 1, pltpu.roll(grads, size - 1, 0), 0.0)
            further = jnp.where(row < size - 2, pltpu.roll(grads, size - 2, 0), 0.0)
            result = grads * weight[0:1] + ahead * weight[1:2] + further * weight[2:3]
            grad_ref[part, :, lanes] = result.astype(jnp.bfloat16)
            first_ref[part, :, lanes] = grads[:8]
            last_ref[part, :, lanes] = result[size - 8 :]
            for tap in taps[part]:
                lines.append(jnp.sum(grads * tap, axis=0, keepdims=True) * norm)
        lines.append(jnp.sum(grad_sum * gated, axis=0, keepdims=True) * norm)
        slopes = slope_ref[block]
        between = slopes[:, LANES:] * carry[:, :LANES] + slopes[:, :LANES] * carry[:, LANES:]
        modes = mode_ref[block]
        lines.append(modes[0:1])
        lines.append(modes[1:2] + jnp.exp(-rate_row) * to_row(between))
        lines.append(jnp.zeros((4, LANES), jnp.float32))
        part_ref[block] = jnp.concatenate(lines, axis=0)


def mend_kernel(grad_ref, last_ref, after_ref, weight_ref, out_ref):
    for part in range(3):
        tile = grad_ref[part]
        last = last_ref[part]
        after = after_ref[part]
        weight = weight_ref[part]
        late = last[6:7] + after[0:1] * weight[2:3]
        final = last[7:8] + after[0:1] * weight[1:2] + after[1:2] * weight[2:3]
        row = iota(tile.shape, 0)
        wide = jnp.where(row == 14, late, jnp.where(row == 15, final, tile.astype(jnp.float32)))
        out_ref[part] = wide.astype(jnp.bfloat16)


def reduce_kernel(
    counts, part_ref, extra_ref, out_ref, near_ref, sum_ref, far_ref, done_ref,
    send_one, recv_one, send_two, recv_two, send_three, recv_three,
):
    dp_count, ctx_count, tp_count = counts
    dp, ctx, tp = lax.axis_index("dp"), lax.axis_index("ctx"), lax.axis_index("tp")
    others = [(a, b) for b in range(tp_count) for a in range(dp_count) if (a, b) != (0, 0)]

    def ring(step):
        return {"ctx": lax.rem(ctx + step, ctx_count)}

    def cross(pair):
        return {"dp": lax.rem(dp + pair[0], dp_count), "tp": lax.rem(tp + pair[1], tp_count)}

    barrier = pltpu.get_barrier_semaphore()
    for step in range(1, ctx_count):
        pl.semaphore_signal(barrier, inc=1, device_id=ring(step), device_id_type=MESH)
    for pair in others:
        pl.semaphore_signal(barrier, inc=1, device_id=cross(pair), device_id_type=MESH)
    pl.semaphore_wait(barrier, ctx_count - 1 + len(others))

    first = []
    for step in range(1, ctx_count):
        first.append(
            pltpu.make_async_remote_copy(
                part_ref.at[lax.rem(ctx + step, ctx_count)], near_ref.at[step],
                send_one.at[step], recv_one.at[step], device_id=ring(step), device_id_type=MESH,
            )
        )
        first[-1].start()
    total = part_ref[ctx] + extra_ref[...]
    for step in range(1, ctx_count):
        first[step - 1].wait_recv()
        total = total + near_ref[step]
    sum_ref[...] = total

    second = []
    for index, pair in enumerate(others):
        second.append(
            pltpu.make_async_remote_copy(
                sum_ref, far_ref.at[index], send_two.at[index], recv_two.at[index],
                device_id=cross(pair), device_id_type=MESH,
            )
        )
        second[-1].start()
    foreign = jnp.zeros_like(total)
    for index, pair in enumerate(others):
        second[index].wait_recv()
        if pair[1] == 0:
            total = total + far_ref[index]
        else:
            foreign = foreign + far_ref[index]
    moved = pltpu.roll(foreign, 2, 1)
    row = iota(total.shape, 1)
    total = jnp.where((row == 12) | (row == 13), moved, total)
    done_ref[...] = total

    third = []
    for step in range(1, ctx_count):
        third.append(
            pltpu.make_async_remote_copy(
                done_ref, out_ref.at[ctx], send_three.at[step], recv_three.at[step],
                device_id=ring(step), device_id_type=MESH,
            )
        )
        third[-1].start()
    out_ref[ctx] = total
    for copy in third:
        copy.wait_recv()
    for copy in first + second + third:
        copy.wait_send()


def local(projected, upstream, short_weight, skip_gain, residues, rates):
    size = projected.shape[1]
    width = projected.shape[3]
    dp_count, ctx_count, tp_count = (lax.axis_size(name) for name in ("dp", "ctx", "tp"))
    block_count = width // LANES
    own_blocks = block_count // ctx_count
    group_count = width // GROUP
    blocks = math.gcd(block_count, 4)
    norm = 1.0 / math.sqrt(dp_count * ctx_count * size)

    proj = projected[0].transpose(1, 0, 2)
    up = upstream[0]
    before = shifted(proj[:, size - 2 :], "ctx", 1)
    tp = lax.axis_index("tp")
    ctx = lax.axis_index("ctx")
    my_rates = lax.dynamic_slice_in_dim(rates, tp * group_count, group_count, 0)
    my_residues = lax.dynamic_slice_in_dim(residues, tp * group_count, group_count, 0)
    rate_rows = my_rates.reshape(block_count, 1, LANES)
    gain_rows = (my_residues * jnp.sqrt(my_rates)).reshape(block_count, 1, LANES)
    own_rates = lax.dynamic_slice_in_dim(rate_rows, ctx * own_blocks, own_blocks, 0)
    skip_row = skip_gain.reshape(1, width)

    grid = (block_count // blocks,)
    step_width = blocks * LANES
    wide3 = pl.BlockSpec((3, size, step_width), lambda i: (0, 0, i))
    halo3 = pl.BlockSpec((3, 2, step_width), lambda i: (0, 0, i))
    tile3 = pl.BlockSpec((3, 8, step_width), lambda i: (0, 0, i))
    taps3 = pl.BlockSpec((3, 3, step_width), lambda i: (0, 0, i))
    flat = pl.BlockSpec((size, step_width), lambda i: (0, i))
    line = pl.BlockSpec((1, step_width), lambda i: (0, i))

    def stacked(rows, cols):
        return pl.BlockSpec((blocks, rows, cols), lambda i: (i, 0, 0))

    def array(*shape, kind=jnp.float32):
        return jax.ShapeDtypeStruct(shape, kind)

    row_spec = stacked(1, LANES)
    params = pltpu.CompilerParams(dimension_semantics=("arbitrary",))

    x, states, slopes = pl.pallas_call(
        functools.partial(gather_kernel, blocks),
        grid=grid,
        in_specs=[wide3, halo3, flat, taps3, row_spec],
        out_specs=[stacked(size, 2 * LANES), stacked(GROUP, 2 * LANES), stacked(GROUP, 2 * LANES)],
        out_shape=[
            array(block_count, size, 2 * LANES, kind=jnp.bfloat16),
            array(block_count, GROUP, 2 * LANES),
            array(block_count, GROUP, 2 * LANES),
        ],
        compiler_params=params,
        name="states",
    )(proj, before, up, short_weight, rate_rows)

    vmem = pl.BlockSpec(memory_space=pltpu.VMEM)
    table = (ctx_count, own_blocks, GROUP, 2 * LANES)
    y, modes, carry, extra = pl.pallas_call(
        functools.partial(exchange_kernel, ctx_count, blocks, block_count // blocks // 2),
        in_specs=[vmem] * 5,
        out_specs=[vmem] * 4,
        out_shape=[
            array(block_count, size, 2 * LANES),
            array(block_count, 8, LANES),
            array(*table),
            array(own_blocks, ROWS, LANES),
        ],
        scratch_shapes=[
            pltpu.VMEM(table, jnp.float32),
            pltpu.VMEM(table, jnp.float32),
            pltpu.SemaphoreType.DMA((ctx_count,)),
            pltpu.SemaphoreType.DMA((ctx_count,)),
            pltpu.SemaphoreType.DMA((ctx_count,)),
            pltpu.SemaphoreType.DMA((ctx_count,)),
        ],
        compiler_params=pltpu.CompilerParams(collective_id=1, has_side_effects=True),
        name="exchange",
    )(states.reshape(table), x, rate_rows, gain_rows, own_rates)
    carry = carry.reshape(block_count, GROUP, 2 * LANES)

    mixed, grad, first, last, part = pl.pallas_call(
        functools.partial(outer_kernel, blocks, norm),
        grid=grid,
        in_specs=[
            wide3, halo3, flat, taps3, line, row_spec, row_spec, stacked(size, 2 * LANES),
            stacked(GROUP, 2 * LANES), stacked(GROUP, 2 * LANES), stacked(8, LANES),
        ],
        out_specs=[flat, wide3, tile3, tile3, stacked(ROWS, LANES)],
        out_shape=[
            array(size, width, kind=jnp.bfloat16),
            array(3, size, width, kind=jnp.bfloat16),
            array(3, 8, width),
            array(3, 8, width),
            array(block_count, ROWS, LANES),
        ],
        compiler_params=params,
        name="outer",
    )(proj, before, up, short_weight, skip_row, rate_rows, gain_rows, y, carry, slopes, modes)

    after = shifted(first[:, :2], "ctx", -1)

    others = dp_count * tp_count - 1
    summed = pl.pallas_call(
        functools.partial(reduce_kernel, (dp_count, ctx_count, tp_count)),
        in_specs=[pl.BlockSpec(memory_space=pltpu.VMEM)] * 2,
        out_specs=pl.BlockSpec(memory_space=pltpu.VMEM),
        out_shape=array(ctx_count, own_blocks, ROWS, LANES),
        scratch_shapes=[
            pltpu.VMEM((ctx_count, own_blocks, ROWS, LANES), jnp.float32),
            pltpu.VMEM((own_blocks, ROWS, LANES), jnp.float32),
            pltpu.VMEM((max(others, 1), own_blocks, ROWS, LANES), jnp.float32),
            pltpu.VMEM((own_blocks, ROWS, LANES), jnp.float32),
            pltpu.SemaphoreType.DMA((ctx_count,)),
            pltpu.SemaphoreType.DMA((ctx_count,)),
            pltpu.SemaphoreType.DMA((max(others, 1),)),
            pltpu.SemaphoreType.DMA((max(others, 1),)),
            pltpu.SemaphoreType.DMA((ctx_count,)),
            pltpu.SemaphoreType.DMA((ctx_count,)),
        ],
        compiler_params=pltpu.CompilerParams(collective_id=0, has_side_effects=True),
        name="reduce",
    )(part.reshape(ctx_count, own_blocks, ROWS, LANES), extra)

    mend_width = math.gcd(width, 1024)
    tail = pl.BlockSpec((3, 16, mend_width), lambda i: (0, size // 16 - 1, i))
    grad = pl.pallas_call(
        mend_kernel,
        grid=(width // mend_width,),
        in_specs=[
            tail,
            pl.BlockSpec((3, 8, mend_width), lambda i: (0, 0, i)),
            pl.BlockSpec((3, 2, mend_width), lambda i: (0, 0, i)),
            pl.BlockSpec((3, 3, mend_width), lambda i: (0, 0, i)),
        ],
        out_specs=tail,
        out_shape=array(3, size, width, kind=jnp.bfloat16),
        input_output_aliases={0: 0},
        compiler_params=params,
        name="mend",
    )(grad, last, after, short_weight)

    flat_sums = summed.reshape(block_count, ROWS, LANES)
    grad_short = flat_sums[:, :9].transpose(1, 0, 2).reshape(3, 3, width)
    grad_skip = flat_sums[:, 9].reshape(width)

    def both_halves(index):
        mine = flat_sums[:, 10 + index].reshape(1, group_count, GROUP)
        if tp_count == 1:
            return mine.reshape(group_count, GROUP)
        other = flat_sums[:, 12 + index].reshape(1, group_count, GROUP)
        low = jnp.where(tp == 0, mine, other)
        high = jnp.where(tp == 0, other, mine)
        return jnp.concatenate([low, high], axis=0).reshape(2 * group_count, GROUP)

    sum_plain = both_halves(0)
    sum_weighted = both_halves(1)
    root = jnp.sqrt(rates)
    grad_residues = root * sum_plain * norm
    grad_log_rates = residues * (0.5 * root * sum_plain - rates * root * sum_weighted) * norm
    return (
        mixed[None],
        grad.transpose(1, 0, 2)[None],
        grad_short,
        grad_skip,
        grad_residues,
        grad_log_rates,
    )


def solution(mesh):
    in_specs = (
        P("dp", "ctx", None, "tp"),
        P("dp", "ctx", "tp"),
        P(None, None, "tp"),
        P("tp"),
        P(),
        P(),
    )
    out_specs = (
        P("dp", "ctx", "tp"),
        P("dp", "ctx", None, "tp"),
        P(None, None, "tp"),
        P("tp"),
        P(),
        P(),
    )
    return jax.shard_map(local, mesh=mesh, in_specs=in_specs, out_specs=out_specs, check_vma=False)
```

```python
import functools
import math

import jax
import jax.numpy as jnp
from jax import lax
from jax.experimental import pallas as pl
from jax.experimental.pallas import tpu as pltpu
from jax.sharding import PartitionSpec as P

GROUP = 16
LANES = 128
PER_BLOCK = LANES // GROUP
PRECISE = lax.Precision.HIGHEST
MESH = pl.DeviceIdType.MESH
ROWS = 16
SUB = 32


def shifted(value, axis, steps):
    count = lax.axis_size(axis)
    leading, last = (max(0, -steps), min(count, count - steps))
    return lax.ppermute(value, axis, [(source, source + steps) for source in range(leading, last)])


def iota(shape, axis):
    return lax.broadcasted_iota(jnp.int32, shape, axis)


def halves(value):
    high = value.astype(jnp.bfloat16)
    return high, (value - high.astype(jnp.float32)).astype(jnp.bfloat16)


def dot(left, right, dims=((1,), (0,)), precision=None):
    return lax.dot_general(
        left, right, (dims, ((), ())), precision=precision, preferred_element_type=jnp.float32
    )


def flip_matrix(size):
    return (iota((size, size), 0) + iota((size, size), 1) == size - 1).astype(jnp.bfloat16)


def decay_table(rate_row, size):
    ages = (size - 1 - iota((size, LANES), 0)).astype(jnp.float32)
    table = jnp.exp(-(rate_row * ages))
    return table, ages * table


def to_row(value):
    rows = iota((LANES, LANES), 0)
    cols = iota((LANES, LANES), 1)
    same = (rows // GROUP == cols // GROUP).astype(jnp.float32)
    summed = dot(value, same, precision=PRECISE)
    pick = iota(value.shape, 0) == iota(value.shape, 1) % GROUP
    return jnp.sum(jnp.where(pick, summed, 0.0), axis=0, keepdims=True)


def to_wide(rate_row):
    rows = iota((LANES, LANES), 0)
    cols = iota((LANES, LANES), 1)
    same = (rows // GROUP == cols // GROUP).astype(jnp.float32)
    pick = iota((GROUP, LANES), 0) == iota((GROUP, LANES), 1) % GROUP
    return dot(jnp.where(pick, jnp.broadcast_to(rate_row, (GROUP, LANES)), 0.0), same, precision=PRECISE)


def delayed(value, halo):
    row = iota(value.shape, 0)
    one = jnp.where(row == 0, halo[1:2], pltpu.roll(value, 1, 0))
    two = jnp.where(row == 0, halo[0:1], jnp.where(row == 1, halo[1:2], pltpu.roll(value, 2, 0)))
    return one, two


def features_of(proj_ref, halo_ref, weight_ref, lanes):
    outs = []
    taps = []
    for part in range(3):
        now = proj_ref[part, :, lanes].astype(jnp.float32)
        halo = halo_ref[part, :, lanes].astype(jnp.float32)
        one, two = delayed(now, halo)
        weight = weight_ref[part, :, lanes]
        outs.append(now * weight[0:1] + one * weight[1:2] + two * weight[2:3])
        taps.append((now, one, two))
    return outs, taps


def gather_kernel(blocks, proj_ref, halo_ref, up_ref, weight_ref, rate_ref, x_ref, state_ref, slope_ref):
    size = proj_ref.shape[1]
    for block in range(blocks):
        lanes = pl.ds(block * LANES, LANES)
        (query, key, value), _ = features_of(proj_ref, halo_ref, weight_ref, lanes)
        gated = (key * value).astype(jnp.bfloat16)
        grad = (up_ref[:, lanes].astype(jnp.float32) * query).astype(jnp.bfloat16)
        turned = dot(flip_matrix(size), grad).astype(jnp.bfloat16)
        both = jnp.concatenate([gated, turned], axis=1)
        x_ref[block] = both
        table, slope = decay_table(rate_ref[block], size)
        keep = iota((LANES, 2 * LANES), 0) // GROUP == iota((LANES, 2 * LANES), 1) % LANES // GROUP
        for source, target in ((table, state_ref), (slope, slope_ref)):
            high, low = halves(source)
            full = dot(high, both, ((0,), (0,))) + dot(low, both, ((0,), (0,)))
            full = jnp.where(keep, full, 0.0)
            target[block] = jnp.sum(full.reshape(PER_BLOCK, GROUP, 2 * LANES), axis=0)


def inner_blocks(base, blocks, x_ref, rate_ref, gain_ref, y_ref, mode_ref):
    size = x_ref.shape[1]
    runs = size // SUB
    small_keep = iota((PER_BLOCK, LANES), 0) == iota((PER_BLOCK, LANES), 1) // GROUP
    lag_lane = iota((PER_BLOCK, LANES), 1)
    lag_seat = iota((PER_BLOCK, LANES), 0) % runs
    keep = (
        iota((PER_BLOCK * SUB, 2 * LANES), 0) // SUB
        == iota((PER_BLOCK * SUB, 2 * LANES), 1) % LANES // GROUP
    )
    causal = iota((SUB, size), 1) >= iota((SUB, size), 0)
    parity = iota((SUB, LANES), 1) // SUB % 2
    steps = iota((size, LANES), 0).astype(jnp.float32)
    every = range(blocks)
    tables = [decay_table(rate_ref[base + block], size) for block in every]
    taps = []
    for block in every:
        forward = jnp.exp(-(rate_ref[base + block] * steps))
        spread = jnp.where(small_keep, jnp.broadcast_to(gain_ref[base + block], (PER_BLOCK, LANES)), 0.0)
        taps.append(dot(spread, forward, ((1,), (1,)), PRECISE))
    chosen = []
    for block in every:
        picks = []
        for run in range(runs):
            tiled = jnp.concatenate([x_ref[base + block, run * SUB : (run + 1) * SUB]] * PER_BLOCK, axis=0)
            picks.append(jnp.where(keep, tiled, jnp.zeros_like(tiled)))
        chosen.append(picks)

    def stepped(value):
        parts = [value]
        for run in range(1, runs):
            blank = jnp.zeros((run * SUB, value.shape[1]), value.dtype)
            parts.append(jnp.concatenate([blank, value[: size - run * SUB]], axis=0))
        return jnp.concatenate(parts, axis=1)

    crosses = [
        dot(
            stepped(x_ref[base + block, :, LANES:]),
            jnp.concatenate([value[:, :LANES] for value in chosen[block]], axis=1),
            ((1,), (1,)),
        )
        for block in every
    ]
    lefts = []
    for block in every:
        bands = []
        for group in range(PER_BLOCK):
            line = jnp.broadcast_to(taps[block][group : group + 1], (SUB, size))
            line = pltpu.roll(line, 0, 1, stride=1, stride_axis=0)
            bands.append(jnp.where(causal, line, 0.0))
        lefts.append(jnp.concatenate(bands, axis=0).T.astype(jnp.bfloat16))
    for block in every:
        y_ref[base + block] = dot(stepped(lefts[block]), jnp.concatenate(chosen[block], axis=0))
    lags = []
    for block in every:
        packed = []
        for run in range(runs):
            lines = []
            for tile in range(2):
                part = crosses[block][run * SUB : (run + 1) * SUB, tile * LANES : (tile + 1) * LANES]
                two = []
                for odd in range(2):
                    moved = jnp.where(parity == odd, part, 0.0)
                    moved = pltpu.roll(moved, 0, 1, stride=1, stride_axis=0)
                    two.append(jnp.sum(moved, axis=0, keepdims=True))
                lines += [two[0], two[1], two[0], two[1]]
            packed.append(jnp.concatenate(lines, axis=0))
        total = jnp.zeros((PER_BLOCK, LANES), jnp.float32)
        for turn in range(runs):
            lag_run = (lag_seat + turn) % runs
            lines = packed[0]
            for run in range(1, runs):
                lines = jnp.where(lag_run == run, packed[run], lines)
            if turn:
                lines = pltpu.roll(lines, turn * SUB, 1)
            begin = lag_run * SUB
            inside = (lag_lane >= begin) & (lag_lane < begin + 2 * SUB - 1)
            total = total + jnp.where(inside, lines, 0.0)
        lags.append(total)
    spreads = [[dot(lags[block], source, precision=PRECISE) for source in tables[block]] for block in every]
    for block in every:
        outs = [
            jnp.sum(jnp.where(small_keep, spread, 0.0), axis=0, keepdims=True) for spread in spreads[block]
        ]
        mode_ref[base + block] = jnp.concatenate(outs + [jnp.zeros((6, LANES), jnp.float32)], axis=0)


def scan_states(size, ctx, count, recv_ref, rate_ref, carry_ref, extra_ref):
    slots = [lax.rem(ctx - step + count, count) for step in range(count)]
    for block in range(recv_ref.shape[1]):
        rate_row = rate_ref[block]
        decay = jnp.exp(-(to_wide(rate_row) * float(size)))
        held = jnp.zeros((GROUP, LANES), jnp.float32)
        aged = held
        plain = held
        weighted = held
        for step in range(count):
            begin = recv_ref[slots[step], block, :, :LANES]
            other = recv_ref[slots[step], block, :, LANES:]
            carry_ref[step, block, :, :LANES] = held
            plain = plain + other * held
            weighted = weighted + other * aged
            aged = decay * (aged + held)
            held = decay * held + begin
        held = jnp.zeros((GROUP, LANES), jnp.float32)
        for step in reversed(range(count)):
            carry_ref[step, block, :, LANES:] = held
            held = recv_ref[slots[step], block, :, LANES:] + decay * held
        once = jnp.exp(-rate_row)
        extra_ref[block] = jnp.concatenate(
            [
                jnp.zeros((10, LANES), jnp.float32),
                once * to_row(plain),
                once * to_row(plain + float(size) * weighted),
                jnp.zeros((4, LANES), jnp.float32),
            ],
            axis=0,
        )


def exchange_kernel(
    ctx_count, blocks, early, state_ref, x_ref, rate_ref, gain_ref, own_ref, y_ref, mode_ref, carry_ref,
    extra_ref, near_ref, back_ref, send_one, recv_one, send_two, recv_two,
):
    ctx = lax.axis_index("ctx")
    size = x_ref.shape[1]
    rounds = x_ref.shape[0] // blocks

    def peer(step):
        return lax.rem(ctx + step, ctx_count)

    def work(index, carry):
        inner_blocks(index * blocks, blocks, x_ref, rate_ref, gain_ref, y_ref, mode_ref)
        return carry

    barrier = pltpu.get_barrier_semaphore()
    for step in range(1, ctx_count):
        pl.semaphore_signal(barrier, inc=1, device_id={"ctx": peer(step)}, device_id_type=MESH)
    pl.semaphore_wait(barrier, ctx_count - 1)
    first = []
    for step in range(1, ctx_count):
        first.append(
            pltpu.make_async_remote_copy(
                state_ref.at[peer(step)], near_ref.at[step], send_one.at[step], recv_one.at[step],
                device_id={"ctx": peer(step)}, device_id_type=MESH,
            )
        )
        first[-1].start()
    near_ref[0] = state_ref[ctx]
    lax.fori_loop(0, early, work, 0)
    for copy in first:
        copy.wait_recv()
    scan_states(size, ctx, ctx_count, near_ref, own_ref, back_ref, extra_ref)
    second = []
    for step in range(1, ctx_count):
        second.append(
            pltpu.make_async_remote_copy(
                back_ref.at[peer(step)], carry_ref.at[ctx], send_two.at[step], recv_two.at[step],
                device_id={"ctx": peer(step)}, device_id_type=MESH,
            )
        )
        second[-1].start()
    carry_ref[ctx] = back_ref[ctx]
    lax.fori_loop(early, rounds, work, 0)
    for copy in second:
        copy.wait_recv()
    for copy in first + second:
        copy.wait_send()


def outer_kernel(
    counts, blocks, norm, proj_ref, halo_ref, up_ref, weight_ref, skip_ref, rate_ref, gain_ref, y_ref,
    carry_ref, slope_ref, mode_ref, extra_ref, mixed_ref, grad_ref, after_ref, last_ref, out_ref,
    part_ref, head_ref, next_ref, near_ref, sum_ref, far_ref, done_ref, all_ref,
    send_one, recv_one, send_two, recv_two, send_three, recv_three, send_head, recv_head,
):
    dp_count, ctx_count, tp_count = counts
    dp, ctx, tp = lax.axis_index("dp"), lax.axis_index("ctx"), lax.axis_index("tp")
    others = [(a, b) for b in range(tp_count) for a in range(dp_count) if (a, b) != (0, 0)]
    own_blocks = part_ref.shape[1]
    owners = blocks // own_blocks
    index = pl.program_id(0)
    rounds = pl.num_programs(0)
    place = lax.rem(index + ctx // owners, rounds)
    size = proj_ref.shape[1]

    def peer(step):
        return lax.rem(ctx + step, ctx_count)

    def cross(pair):
        return {"dp": lax.rem(dp + pair[0], dp_count), "tp": lax.rem(tp + pair[1], tp_count)}

    barrier = pltpu.get_barrier_semaphore()

    @pl.when(index == 0)
    def _():
        for step in range(1, ctx_count):
            pl.semaphore_signal(barrier, inc=1, device_id={"ctx": peer(step)}, device_id_type=MESH)
        for pair in others:
            pl.semaphore_signal(barrier, inc=1, device_id=cross(pair), device_id_type=MESH)

    row = iota((size, LANES), 0)
    keep = iota((LANES, 2 * LANES), 0) // GROUP == iota((LANES, 2 * LANES), 1) % LANES // GROUP
    ages = (iota((size, LANES), 0) + 1).astype(jnp.float32)
    for block in range(blocks):
        lanes = pl.ds(block * LANES, LANES)
        (query, key, value), taps = features_of(proj_ref, halo_ref, weight_ref, lanes)
        gated = (key * value).astype(jnp.bfloat16).astype(jnp.float32)
        rate_row = rate_ref[block]
        coef = gain_ref[block] * jnp.exp(-(rate_row * ages))
        coef_high, coef_low = halves(coef)
        carry = carry_ref[block]
        spread = jnp.where(keep, jnp.concatenate([carry] * PER_BLOCK, axis=0), 0.0)
        high, low = halves(spread)
        whole = y_ref[block] + (dot(coef_high, high) + (dot(coef_high, low) + dot(coef_low, high)))
        narrow = whole.astype(jnp.bfloat16)
        convolved = narrow[:, :LANES].astype(jnp.float32)
        correlated = dot(flip_matrix(size), narrow[:, LANES:])
        upstream = up_ref[:, lanes].astype(jnp.float32)
        skip = skip_ref[:, lanes]
        grad_sum = upstream * query
        mixture = convolved + skip * gated
        mixed_ref[:, lanes] = (query * mixture).astype(jnp.bfloat16)
        grad_gate = correlated + skip * grad_sum
        lines = []
        heads = []
        lasts = []
        for part, grads in enumerate((upstream * mixture, grad_gate * value, grad_gate * key)):
            weight = weight_ref[part, :, lanes]
            ahead = jnp.where(row < size - 1, pltpu.roll(grads, size - 1, 0), 0.0)
            further = jnp.where(row < size - 2, pltpu.roll(grads, size - 2, 0), 0.0)
            result = grads * weight[0:1] + ahead * weight[1:2] + further * weight[2:3]
            grad_ref[part, :, lanes] = result.astype(jnp.bfloat16)
            heads.append(grads[:2])
            lasts.append(result[size - 2 :])
            for tap in taps[part]:
                lines.append(jnp.sum(grads * tap, axis=0, keepdims=True) * norm)
        blank = jnp.zeros((2, LANES), jnp.float32)
        head_ref[index, :, lanes] = jnp.concatenate(heads + [blank], axis=0)
        last_ref[:, lanes] = jnp.concatenate(lasts + [blank], axis=0)
        lines.append(jnp.sum(grad_sum * gated, axis=0, keepdims=True) * norm)
        slopes = slope_ref[block]
        between = slopes[:, LANES:] * carry[:, :LANES] + slopes[:, :LANES] * carry[:, LANES:]
        modes = mode_ref[block]
        lines.append(modes[0:1])
        lines.append(modes[1:2] + jnp.exp(-rate_row) * to_row(between))
        lines.append(jnp.zeros((4, LANES), jnp.float32))
        part_ref[place * owners + block // own_blocks, block % own_blocks] = jnp.concatenate(lines, axis=0)

    @pl.when(index == 0)
    def _():
        pl.semaphore_wait(barrier, ctx_count - 1 + len(others))

    def first_copy(owner, source):
        return pltpu.make_async_remote_copy(
            part_ref.at[owner], near_ref.at[source], send_one.at[owner], recv_one.at[source],
            device_id={"ctx": owner}, device_id_type=MESH,
        )

    def head_copy(at):
        return pltpu.make_async_remote_copy(
            head_ref.at[at], next_ref.at[at], send_head.at[at], recv_head.at[at],
            device_id={"ctx": lax.rem(ctx + ctx_count - 1, ctx_count)}, device_id_type=MESH,
        )

    for item in range(owners):
        owner = place * owners + item

        @pl.when(owner != ctx)
        def _():
            first_copy(owner, ctx).start()

    head_copy(index).start()

    @pl.when(index == rounds - 1)
    def _():
        total = part_ref[ctx] + extra_ref[...]
        for step in range(1, ctx_count):
            first_copy(ctx, peer(step)).wait_recv()
            total = total + near_ref[peer(step)]
        sum_ref[...] = total
        second = []
        for number, pair in enumerate(others):
            second.append(
                pltpu.make_async_remote_copy(
                    sum_ref, far_ref.at[number], send_two.at[number], recv_two.at[number],
                    device_id=cross(pair), device_id_type=MESH,
                )
            )
            second[-1].start()
        foreign = jnp.zeros_like(total)
        for number, pair in enumerate(others):
            second[number].wait_recv()
            if pair[1] == 0:
                total = total + far_ref[number]
            else:
                foreign = foreign + far_ref[number]
        line = iota(total.shape, 1)
        low = jnp.where(tp == 0, total, foreign)
        high = pltpu.roll(jnp.where(tp == 0, foreign, total), 2, 1)
        total = jnp.where(line < 10, total, jnp.where(line < 12, low, high))
        done_ref[...] = total
        third = []
        for step in range(1, ctx_count):
            third.append(
                pltpu.make_async_remote_copy(
                    done_ref, all_ref.at[ctx], send_three.at[step], recv_three.at[step],
                    device_id={"ctx": peer(step)}, device_id_type=MESH,
                )
            )
            third[-1].start()
        all_ref[ctx] = total
        width = blocks * LANES
        for at in range(part_ref.shape[0] // owners):
            head_copy(at).wait_recv()
            spot = lax.rem(at + lax.rem(ctx + 1, ctx_count) // owners, part_ref.shape[0] // owners)
            rows = next_ref[at]
            after_ref[:, pl.ds(pl.multiple_of(spot * width, LANES), width)] = jnp.where(
                ctx < ctx_count - 1, rows, jnp.zeros_like(rows)
            )
        for copy in third:
            copy.wait_recv()
        out_ref[...] = all_ref[...]
        for step in range(1, ctx_count):
            first_copy(peer(step), ctx).wait_send()
        for at in range(part_ref.shape[0] // owners):
            head_copy(at).wait_send()
        for copy in second + third:
            copy.wait_send()


def finish_kernel(
    blocks, grad_ref, mixed_ref, after_ref, last_ref, weight_ref, sum_ref, grad_out, mixed_out, short_out,
    skip_out,
):
    mixed_out[...] = mixed_ref[...]
    size = grad_ref.shape[1]
    for part in range(3):
        weight = weight_ref[part]
        after = after_ref[2 * part : 2 * part + 2]
        late = last_ref[2 * part : 2 * part + 1] + after[0:1] * weight[2:3]
        final = last_ref[2 * part + 1 : 2 * part + 2] + after[0:1] * weight[1:2] + after[1:2] * weight[2:3]
        grad_out[part, : size - 16] = grad_ref[part, : size - 16]
        tile = grad_ref[part, size - 16 :].astype(jnp.float32)
        row = iota(tile.shape, 0)
        tile = jnp.where(row == 14, late, jnp.where(row == 15, final, tile))
        grad_out[part, size - 16 :] = tile.astype(jnp.bfloat16)
    for block in range(blocks):
        lanes = pl.ds(block * LANES, LANES)
        for part in range(3):
            short_out[part, :, lanes] = sum_ref[block, 3 * part : 3 * part + 3]
        skip_out[:, lanes] = sum_ref[block, 9:10]


def local(projected, upstream, short_weight, skip_gain, residues, rates):
    size = projected.shape[1]
    width = projected.shape[3]
    dp_count, ctx_count, tp_count = (lax.axis_size(name) for name in ("dp", "ctx", "tp"))
    block_count = width // LANES
    own_blocks = block_count // ctx_count
    group_count = width // GROUP
    blocks = math.gcd(block_count, 4)
    norm = 1.0 / math.sqrt(dp_count * ctx_count * size)

    proj = projected[0].transpose(1, 0, 2)
    up = upstream[0]
    before = shifted(proj[:, size - 2 :], "ctx", 1)
    tp = lax.axis_index("tp")
    ctx = lax.axis_index("ctx")
    my_rates = lax.dynamic_slice_in_dim(rates, tp * group_count, group_count, 0)
    my_residues = lax.dynamic_slice_in_dim(residues, tp * group_count, group_count, 0)
    rate_rows = my_rates.reshape(block_count, 1, LANES)
    gain_rows = (my_residues * jnp.sqrt(my_rates)).reshape(block_count, 1, LANES)
    own_rates = lax.dynamic_slice_in_dim(rate_rows, ctx * own_blocks, own_blocks, 0)
    skip_row = skip_gain.reshape(1, width)

    grid = (block_count // blocks,)
    step_width = blocks * LANES
    wide3 = pl.BlockSpec((3, size, step_width), lambda i: (0, 0, i))
    halo3 = pl.BlockSpec((3, 2, step_width), lambda i: (0, 0, i))
    taps3 = pl.BlockSpec((3, 3, step_width), lambda i: (0, 0, i))
    flat = pl.BlockSpec((size, step_width), lambda i: (0, i))
    line = pl.BlockSpec((1, step_width), lambda i: (0, i))

    def stacked(rows, cols):
        return pl.BlockSpec((blocks, rows, cols), lambda i: (i, 0, 0))

    def array(*shape, kind=jnp.float32):
        return jax.ShapeDtypeStruct(shape, kind)

    row_spec = stacked(1, LANES)
    params = pltpu.CompilerParams(dimension_semantics=("arbitrary",))

    x, states, slopes = pl.pallas_call(
        functools.partial(gather_kernel, blocks),
        grid=grid,
        in_specs=[wide3, halo3, flat, taps3, row_spec],
        out_specs=[stacked(size, 2 * LANES), stacked(GROUP, 2 * LANES), stacked(GROUP, 2 * LANES)],
        out_shape=[
            array(block_count, size, 2 * LANES, kind=jnp.bfloat16),
            array(block_count, GROUP, 2 * LANES),
            array(block_count, GROUP, 2 * LANES),
        ],
        compiler_params=params,
        name="states",
    )(proj, before, up, short_weight, rate_rows)

    vmem = pl.BlockSpec(memory_space=pltpu.VMEM)
    table = (ctx_count, own_blocks, GROUP, 2 * LANES)
    y, modes, carry, extra = pl.pallas_call(
        functools.partial(exchange_kernel, ctx_count, blocks, block_count // blocks // 2),
        in_specs=[vmem] * 5,
        out_specs=[vmem] * 4,
        out_shape=[
            array(block_count, size, 2 * LANES),
            array(block_count, 8, LANES),
            array(*table),
            array(own_blocks, ROWS, LANES),
        ],
        scratch_shapes=[
            pltpu.VMEM(table, jnp.float32),
            pltpu.VMEM(table, jnp.float32),
            pltpu.SemaphoreType.DMA((ctx_count,)),
            pltpu.SemaphoreType.DMA((ctx_count,)),
            pltpu.SemaphoreType.DMA((ctx_count,)),
            pltpu.SemaphoreType.DMA((ctx_count,)),
        ],
        compiler_params=pltpu.CompilerParams(collective_id=1, has_side_effects=True),
        name="exchange",
    )(states.reshape(table), x, rate_rows, gain_rows, own_rates)
    carry = carry.reshape(block_count, GROUP, 2 * LANES)

    owners = blocks // own_blocks
    rounds = block_count // blocks
    others = max(dp_count * tp_count - 1, 1)
    own = (own_blocks, ROWS, LANES)

    def turned(rank, at):
        def index_map(i):
            spot = lax.rem(i + lax.axis_index("ctx") // owners, rounds)
            return tuple(spot if d == at else 0 for d in range(rank))

        return index_map

    def lane_spec(*shape):
        return pl.BlockSpec(shape + (step_width,), turned(len(shape) + 1, len(shape)))

    def block_spec(rows, cols):
        return pl.BlockSpec((blocks, rows, cols), turned(3, 0))

    def whole(*shape):
        return pl.BlockSpec(shape, lambda i: (0,) * len(shape))

    mixed, grad, after, last, summed = pl.pallas_call(
        functools.partial(outer_kernel, (dp_count, ctx_count, tp_count), blocks, norm),
        grid=grid,
        in_specs=[
            lane_spec(3, size), lane_spec(3, 2), lane_spec(size), lane_spec(3, 3), lane_spec(1),
            block_spec(1, LANES), block_spec(1, LANES), block_spec(size, 2 * LANES),
            block_spec(GROUP, 2 * LANES), block_spec(GROUP, 2 * LANES), block_spec(8, LANES),
            whole(*own),
        ],
        out_specs=[
            lane_spec(size), lane_spec(3, size), whole(8, width), lane_spec(8), whole(ctx_count, *own)
        ],
        out_shape=[
            array(size, width, kind=jnp.bfloat16),
            array(3, size, width, kind=jnp.bfloat16),
            array(8, width),
            array(8, width),
            array(ctx_count, *own),
        ],
        scratch_shapes=[
            pltpu.VMEM((ctx_count,) + own, jnp.float32),
            pltpu.VMEM((rounds, 8, step_width), jnp.float32),
            pltpu.VMEM((rounds, 8, step_width), jnp.float32),
            pltpu.VMEM((ctx_count,) + own, jnp.float32),
            pltpu.VMEM(own, jnp.float32),
            pltpu.VMEM((others,) + own, jnp.float32),
            pltpu.VMEM(own, jnp.float32),
            pltpu.VMEM((ctx_count,) + own, jnp.float32),
            pltpu.SemaphoreType.DMA((ctx_count,)),
            pltpu.SemaphoreType.DMA((ctx_count,)),
            pltpu.SemaphoreType.DMA((others,)),
            pltpu.SemaphoreType.DMA((others,)),
            pltpu.SemaphoreType.DMA((ctx_count,)),
            pltpu.SemaphoreType.DMA((ctx_count,)),
            pltpu.SemaphoreType.DMA((rounds,)),
            pltpu.SemaphoreType.DMA((rounds,)),
        ],
        compiler_params=pltpu.CompilerParams(
            dimension_semantics=("arbitrary",), collective_id=0, has_side_effects=True
        ),
        name="outer",
    )(proj, before, up, short_weight, skip_row, rate_rows, gain_rows, y, carry, slopes, modes, extra)
    summed = summed.reshape(block_count, ROWS, LANES)

    eight = pl.BlockSpec((8, step_width), lambda i: (0, i))
    grad, mixed, grad_short, grad_skip = pl.pallas_call(
        functools.partial(finish_kernel, blocks),
        grid=grid,
        in_specs=[wide3, flat, eight, eight, taps3, stacked(ROWS, LANES)],
        out_specs=[wide3, flat, taps3, line],
        out_shape=[
            array(3, size, width, kind=jnp.bfloat16),
            array(size, width, kind=jnp.bfloat16),
            array(3, 3, width),
            array(1, width),
        ],
        compiler_params=params,
        name="finish",
    )(grad, mixed, after, last, short_weight, summed)

    modes = summed[:, 10 : 10 + 2 * tp_count].reshape(block_count, tp_count, 2, PER_BLOCK, GROUP)
    sum_plain, sum_weighted = (
        modes[:, :, index].transpose(1, 0, 2, 3).reshape(tp_count * group_count, GROUP) for index in range(2)
    )
    root = jnp.sqrt(rates)
    grad_residues = root * sum_plain * norm
    grad_log_rates = residues * (0.5 * root * sum_plain - rates * root * sum_weighted) * norm
    return (
        mixed[None],
        grad.transpose(1, 0, 2)[None],
        grad_short,
        grad_skip.reshape(width),
        grad_residues,
        grad_log_rates,
    )


def solution(mesh):
    in_specs = (
        P("dp", "ctx", None, "tp"),
        P("dp", "ctx", "tp"),
        P(None, None, "tp"),
        P("tp"),
        P(),
        P(),
    )
    out_specs = (
        P("dp", "ctx", "tp"),
        P("dp", "ctx", None, "tp"),
        P(None, None, "tp"),
        P("tp"),
        P(),
        P(),
    )
    return jax.shard_map(local, mesh=mesh, in_specs=in_specs, out_specs=out_specs, check_vma=False)
```

```python
import functools
import math

import jax
import jax.numpy as jnp
from jax import lax
from jax.experimental import pallas as pl
from jax.experimental.pallas import tpu as pltpu
from jax.sharding import PartitionSpec as P

GROUP = 16
LANES = 128
PER_BLOCK = LANES // GROUP
MESH = pl.DeviceIdType.MESH
ROWS = 16
SUB = 32


def shifted(value, axis, steps):
    count = lax.axis_size(axis)
    leading, last = (max(0, -steps), min(count, count - steps))
    return lax.ppermute(value, axis, [(source, source + steps) for source in range(leading, last)])


def iota(shape, axis):
    return lax.broadcasted_iota(jnp.int32, shape, axis)


def halves(value):
    high = value.astype(jnp.bfloat16)
    return high, (value - high.astype(jnp.float32)).astype(jnp.bfloat16)


def thirds(value):
    high = value.astype(jnp.bfloat16)
    rest = value - high.astype(jnp.float32)
    middle = rest.astype(jnp.bfloat16)
    return high, middle, (rest - middle.astype(jnp.float32)).astype(jnp.bfloat16)


def dot(left, right, dims=((1,), (0,)), precision=None):
    return lax.dot_general(
        left, right, (dims, ((), ())), precision=precision, preferred_element_type=jnp.float32
    )


def flip_matrix(size):
    return (iota((size, size), 0) + iota((size, size), 1) == size - 1).astype(jnp.bfloat16)


def decay_table(rate_row, size):
    ages = (size - 1 - iota((size, LANES), 0)).astype(jnp.float32)
    table = jnp.exp(-(rate_row * ages))
    return table, ages * table


def group_dot(value):
    rows = iota((3 * LANES, LANES), 0)
    cols = iota((3 * LANES, LANES), 1)
    same = (rows % LANES // GROUP == cols // GROUP).astype(jnp.bfloat16)
    return dot(jnp.concatenate(thirds(value), axis=1), same)


def to_row(value):
    pick = iota(value.shape, 0) == iota(value.shape, 1) % GROUP
    return jnp.sum(jnp.where(pick, group_dot(value), 0.0), axis=0, keepdims=True)


def to_wide(rate_row):
    pick = iota((GROUP, LANES), 0) == iota((GROUP, LANES), 1) % GROUP
    return group_dot(jnp.where(pick, jnp.broadcast_to(rate_row, (GROUP, LANES)), 0.0))


def features_of(proj_ref, halo_ref, weight_ref, pad_ref, lanes, zero):
    outs = []
    taps = []
    size = proj_ref.shape[1]
    for part in range(3):
        now = proj_ref[part, :, lanes].astype(jnp.float32)
        halo = halo_ref[part, :, lanes].astype(jnp.float32)
        pad_ref[part, 0:8] = jnp.concatenate([jnp.zeros((6, LANES), jnp.float32), halo], axis=0)
        pad_ref[part, 8:] = now
        one = pad_ref[part, pl.ds(zero + 7, size)]
        two = pad_ref[part, pl.ds(zero + 6, size)]
        weight = weight_ref[part, :, lanes]
        outs.append(now * weight[0:1] + one * weight[1:2] + two * weight[2:3])
        taps.append((now, one, two))
    return outs, taps


def gather_kernel(blocks, proj_ref, halo_ref, up_ref, weight_ref, rate_ref, x_ref, state_ref, slope_ref, pad_ref):
    size = proj_ref.shape[1]
    zero = jnp.minimum(pl.program_id(0), 0)
    keep = iota((LANES, 2 * LANES), 0) // GROUP == iota((LANES, 2 * LANES), 1) % LANES // GROUP
    tables = [
        [halves(source) for source in decay_table(rate_ref[block], size)] for block in range(blocks)
    ]
    pairs = []
    for block in range(blocks):
        lanes = pl.ds(block * LANES, LANES)
        (query, key, value), _ = features_of(proj_ref, halo_ref, weight_ref, pad_ref.at[block], lanes, zero)
        gated = (key * value).astype(jnp.bfloat16)
        grad = (up_ref[:, lanes].astype(jnp.float32) * query).astype(jnp.bfloat16)
        pairs.append((gated, grad))
    boths = []
    for block in range(blocks):
        gated, grad = pairs[block]
        boths.append(jnp.concatenate([gated, dot(flip_matrix(size), grad).astype(jnp.bfloat16)], axis=1))
        x_ref[block] = boths[-1]
    for block in range(blocks):
        for (high, low), target in zip(tables[block], (state_ref, slope_ref)):
            full = dot(
                jnp.concatenate([high, low], axis=0),
                jnp.concatenate([boths[block], boths[block]], axis=0),
                ((0,), (0,)),
            )
            full = jnp.where(keep, full, 0.0)
            target[block] = jnp.sum(full.reshape(PER_BLOCK, GROUP, 2 * LANES), axis=0)


def inner_blocks(base, blocks, x_ref, rate_ref, gain_ref, y_ref, mode_ref):
    size = x_ref.shape[1]
    runs = size // SUB
    small_keep = iota((PER_BLOCK, LANES), 0) == iota((PER_BLOCK, LANES), 1) // GROUP
    wide_keep = iota((PER_BLOCK, 2 * LANES), 0) == iota((PER_BLOCK, 2 * LANES), 1) % LANES // GROUP
    lag_lane = iota((PER_BLOCK, LANES), 1)
    lag_seat = iota((PER_BLOCK, LANES), 0) % runs
    keep = (
        iota((PER_BLOCK * SUB, 2 * LANES), 0) // SUB
        == iota((PER_BLOCK * SUB, 2 * LANES), 1) % LANES // GROUP
    )
    causal = iota((SUB, size), 1) >= iota((SUB, size), 0)
    parity = iota((SUB, LANES), 1) // SUB % 2
    steps = iota((size, LANES), 0).astype(jnp.float32)
    every = range(blocks)
    tables = [decay_table(rate_ref[base + block], size) for block in every]
    taps = []
    for block in every:
        forward = jnp.exp(-(rate_ref[base + block] * steps))
        spread = jnp.where(small_keep, jnp.broadcast_to(gain_ref[base + block], (PER_BLOCK, LANES)), 0.0)
        a, b, c = thirds(spread)
        d, e, f = thirds(forward)
        taps.append(
            dot(
                jnp.concatenate([a, a, b, a, b, c], axis=1),
                jnp.concatenate([d, e, d, f, e, d], axis=1),
                ((1,), (1,)),
            )
        )
    chosen = []
    for block in every:
        picks = []
        for run in range(runs):
            tiled = jnp.concatenate([x_ref[base + block, run * SUB : (run + 1) * SUB]] * PER_BLOCK, axis=0)
            picks.append(jnp.where(keep, tiled, jnp.zeros_like(tiled)))
        chosen.append(picks)

    def stepped(value):
        parts = [value]
        for run in range(1, runs):
            blank = jnp.zeros((run * SUB, value.shape[1]), value.dtype)
            parts.append(jnp.concatenate([blank, value[: size - run * SUB]], axis=0))
        return jnp.concatenate(parts, axis=1)

    crosses = [
        dot(
            stepped(x_ref[base + block, :, LANES:]),
            jnp.concatenate([value[:, :LANES] for value in chosen[block]], axis=1),
            ((1,), (1,)),
        )
        for block in every
    ]
    lefts = []
    for block in every:
        bands = []
        for group in range(PER_BLOCK):
            line = jnp.broadcast_to(taps[block][group : group + 1], (SUB, size))
            line = pltpu.roll(line, 0, 1, stride=1, stride_axis=0)
            bands.append(jnp.where(causal, line, 0.0))
        lefts.append(jnp.concatenate(bands, axis=0).T.astype(jnp.bfloat16))
    for block in every:
        y_ref[base + block] = dot(stepped(lefts[block]), jnp.concatenate(chosen[block], axis=0))
    lags = []
    for block in every:
        packed = []
        for run in range(runs):
            lines = []
            for tile in range(2):
                part = crosses[block][run * SUB : (run + 1) * SUB, tile * LANES : (tile + 1) * LANES]
                two = []
                for odd in range(2):
                    moved = jnp.where(parity == odd, part, 0.0)
                    moved = pltpu.roll(moved, 0, 1, stride=1, stride_axis=0)
                    two.append(jnp.sum(moved, axis=0, keepdims=True))
                lines += [two[0], two[1], two[0], two[1]]
            packed.append(jnp.concatenate(lines, axis=0))
        total = jnp.zeros((PER_BLOCK, LANES), jnp.float32)
        for turn in range(runs):
            lag_run = (lag_seat + turn) % runs
            lines = packed[0]
            for run in range(1, runs):
                lines = jnp.where(lag_run == run, packed[run], lines)
            if turn:
                lines = pltpu.roll(lines, turn * SUB, 1)
            begin = lag_run * SUB
            inside = (lag_lane >= begin) & (lag_lane < begin + 2 * SUB - 1)
            total = total + jnp.where(inside, lines, 0.0)
        lags.append(total)
    for block in every:
        high, low = halves(lags[block])
        table_high, table_low = halves(jnp.concatenate(tables[block], axis=1))
        spread = dot(
            jnp.concatenate([high, high, low], axis=1),
            jnp.concatenate([table_high, table_low, table_high], axis=0),
        )
        spread = jnp.where(wide_keep, spread, 0.0)
        line = jnp.sum(spread, axis=0, keepdims=True)
        mode_ref[base + block] = jnp.concatenate(
            [line[:, :LANES], line[:, LANES:], jnp.zeros((6, LANES), jnp.float32)], axis=0
        )


def scan_states(size, ctx, count, recv_ref, rate_ref, carry_ref, extra_ref):
    slots = [lax.rem(ctx - step + count, count) for step in range(count)]
    for block in range(recv_ref.shape[1]):
        rate_row = rate_ref[block]
        decay = jnp.exp(-(to_wide(rate_row) * float(size)))
        held = jnp.zeros((GROUP, LANES), jnp.float32)
        aged = held
        plain = held
        weighted = held
        for step in range(count):
            begin = recv_ref[slots[step], block, :, :LANES]
            other = recv_ref[slots[step], block, :, LANES:]
            carry_ref[step, block, :, :LANES] = held
            plain = plain + other * held
            weighted = weighted + other * aged
            aged = decay * (aged + held)
            held = decay * held + begin
        held = jnp.zeros((GROUP, LANES), jnp.float32)
        for step in reversed(range(count)):
            carry_ref[step, block, :, LANES:] = held
            held = recv_ref[slots[step], block, :, LANES:] + decay * held
        once = jnp.exp(-rate_row)
        extra_ref[block] = jnp.concatenate(
            [
                jnp.zeros((10, LANES), jnp.float32),
                once * to_row(plain),
                once * to_row(plain + float(size) * weighted),
                jnp.zeros((4, LANES), jnp.float32),
            ],
            axis=0,
        )


def exchange_kernel(
    ctx_count, blocks, early, state_ref, x_ref, rate_ref, gain_ref, own_ref, y_ref, mode_ref, carry_ref,
    extra_ref, near_ref, back_ref, send_one, recv_one, send_two, recv_two,
):
    ctx = lax.axis_index("ctx")
    size = x_ref.shape[1]
    rounds = x_ref.shape[0] // blocks

    def peer(step):
        return lax.rem(ctx + step, ctx_count)

    def work(index, carry):
        inner_blocks(index * blocks, blocks, x_ref, rate_ref, gain_ref, y_ref, mode_ref)
        return carry

    barrier = pltpu.get_barrier_semaphore()
    for step in range(1, ctx_count):
        pl.semaphore_signal(barrier, inc=1, device_id={"ctx": peer(step)}, device_id_type=MESH)
    pl.semaphore_wait(barrier, ctx_count - 1)
    first = []
    for step in range(1, ctx_count):
        first.append(
            pltpu.make_async_remote_copy(
                state_ref.at[peer(step)], near_ref.at[step], send_one.at[step], recv_one.at[step],
                device_id={"ctx": peer(step)}, device_id_type=MESH,
            )
        )
        first[-1].start()
    near_ref[0] = state_ref[ctx]
    lax.fori_loop(0, early, work, 0)
    for copy in first:
        copy.wait_recv()
    scan_states(size, ctx, ctx_count, near_ref, own_ref, back_ref, extra_ref)
    second = []
    for step in range(1, ctx_count):
        second.append(
            pltpu.make_async_remote_copy(
                back_ref.at[peer(step)], carry_ref.at[ctx], send_two.at[step], recv_two.at[step],
                device_id={"ctx": peer(step)}, device_id_type=MESH,
            )
        )
        second[-1].start()
    carry_ref[ctx] = back_ref[ctx]
    lax.fori_loop(early, rounds, work, 0)
    for copy in second:
        copy.wait_recv()
    for copy in first + second:
        copy.wait_send()


def outer_kernel(
    counts, blocks, norm, proj_ref, halo_ref, up_ref, weight_ref, skip_ref, rate_ref, gain_ref, y_ref,
    carry_ref, slope_ref, mode_ref, extra_ref, mixed_ref, grad_ref, after_ref, last_ref, out_ref,
    pad_ref, tail_ref, part_ref, head_ref, next_ref, near_ref, sum_ref, far_ref, done_ref, all_ref,
    send_one, recv_one, send_two, recv_two, send_three, recv_three, send_head, recv_head,
):
    dp_count, ctx_count, tp_count = counts
    dp, ctx, tp = lax.axis_index("dp"), lax.axis_index("ctx"), lax.axis_index("tp")
    others = [(a, b) for b in range(tp_count) for a in range(dp_count) if (a, b) != (0, 0)]
    own_blocks = part_ref.shape[1]
    owners = blocks // own_blocks
    index = pl.program_id(0)
    rounds = pl.num_programs(0)
    place = lax.rem(index + ctx // owners, rounds)
    size = proj_ref.shape[1]

    def peer(step):
        return lax.rem(ctx + step, ctx_count)

    def cross(pair):
        return {"dp": lax.rem(dp + pair[0], dp_count), "tp": lax.rem(tp + pair[1], tp_count)}

    barrier = pltpu.get_barrier_semaphore()

    @pl.when(index == 0)
    def _():
        for step in range(1, ctx_count):
            pl.semaphore_signal(barrier, inc=1, device_id={"ctx": peer(step)}, device_id_type=MESH)
        for pair in others:
            pl.semaphore_signal(barrier, inc=1, device_id=cross(pair), device_id_type=MESH)

    zero = jnp.minimum(index, 0)
    keep = iota((LANES, 2 * LANES), 0) // GROUP == iota((LANES, 2 * LANES), 1) % LANES // GROUP
    ages = (iota((size, LANES), 0) + 1).astype(jnp.float32)
    for block in range(blocks):
        lanes = pl.ds(block * LANES, LANES)
        (query, key, value), taps = features_of(proj_ref, halo_ref, weight_ref, pad_ref.at[block], lanes, zero)
        gated = (key * value).astype(jnp.bfloat16).astype(jnp.float32)
        rate_row = rate_ref[block]
        coef = gain_ref[block] * jnp.exp(-(rate_row * ages))
        coef_high, coef_low = halves(coef)
        carry = carry_ref[block]
        high, low = (
            jnp.where(keep, jnp.concatenate([value] * PER_BLOCK, axis=0), jnp.zeros((), jnp.bfloat16))
            for value in halves(carry)
        )
        whole = y_ref[block] + dot(
            jnp.concatenate([coef_high, coef_high, coef_low], axis=1),
            jnp.concatenate([high, low, high], axis=0),
        )
        narrow = whole.astype(jnp.bfloat16)
        convolved = narrow[:, :LANES].astype(jnp.float32)
        correlated = dot(flip_matrix(size), narrow[:, LANES:])
        upstream = up_ref[:, lanes].astype(jnp.float32)
        skip = skip_ref[:, lanes]
        grad_sum = upstream * query
        mixture = convolved + skip * gated
        mixed_ref[:, lanes] = (query * mixture).astype(jnp.bfloat16)
        grad_gate = correlated + skip * grad_sum
        lines = []
        heads = []
        lasts = []
        for part, grads in enumerate((upstream * mixture, grad_gate * value, grad_gate * key)):
            weight = weight_ref[part, :, lanes]
            tail_ref[block, part, :size] = grads
            tail_ref[block, part, size:] = jnp.zeros((8, LANES), jnp.float32)
            ahead = tail_ref[block, part, pl.ds(zero + 1, size)]
            further = tail_ref[block, part, pl.ds(zero + 2, size)]
            result = grads * weight[0:1] + ahead * weight[1:2] + further * weight[2:3]
            grad_ref[part, :, lanes] = result.astype(jnp.bfloat16)
            heads.append(grads[:2])
            lasts.append(result[size - 2 :])
            for tap in taps[part]:
                lines.append(jnp.sum(grads * tap, axis=0, keepdims=True) * norm)
        blank = jnp.zeros((2, LANES), jnp.float32)
        head_ref[index, :, lanes] = jnp.concatenate(heads + [blank], axis=0)
        last_ref[:, lanes] = jnp.concatenate(lasts + [blank], axis=0)
        lines.append(jnp.sum(grad_sum * gated, axis=0, keepdims=True) * norm)
        slopes = slope_ref[block]
        between = slopes[:, LANES:] * carry[:, :LANES] + slopes[:, :LANES] * carry[:, LANES:]
        modes = mode_ref[block]
        lines.append(modes[0:1])
        lines.append(modes[1:2] + jnp.exp(-rate_row) * to_row(between))
        lines.append(jnp.zeros((4, LANES), jnp.float32))
        part_ref[place * owners + block // own_blocks, block % own_blocks] = jnp.concatenate(lines, axis=0)

    @pl.when(index == 0)
    def _():
        pl.semaphore_wait(barrier, ctx_count - 1 + len(others))

    def first_copy(owner, source):
        return pltpu.make_async_remote_copy(
            part_ref.at[owner], near_ref.at[source], send_one.at[owner], recv_one.at[source],
            device_id={"ctx": owner}, device_id_type=MESH,
        )

    def head_copy(at):
        return pltpu.make_async_remote_copy(
            head_ref.at[at], next_ref.at[at], send_head.at[at], recv_head.at[at],
            device_id={"ctx": lax.rem(ctx + ctx_count - 1, ctx_count)}, device_id_type=MESH,
        )

    for item in range(owners):
        owner = place * owners + item

        @pl.when(owner != ctx)
        def _():
            first_copy(owner, ctx).start()

    head_copy(index).start()

    @pl.when(index == rounds - 1)
    def _():
        total = part_ref[ctx] + extra_ref[...]
        for step in range(1, ctx_count):
            first_copy(ctx, peer(step)).wait_recv()
            total = total + near_ref[peer(step)]
        sum_ref[...] = total
        second = []
        for number, pair in enumerate(others):
            second.append(
                pltpu.make_async_remote_copy(
                    sum_ref, far_ref.at[number], send_two.at[number], recv_two.at[number],
                    device_id=cross(pair), device_id_type=MESH,
                )
            )
            second[-1].start()
        foreign = jnp.zeros_like(total)
        for number, pair in enumerate(others):
            second[number].wait_recv()
            if pair[1] == 0:
                total = total + far_ref[number]
            else:
                foreign = foreign + far_ref[number]
        line = iota(total.shape, 1)
        low = jnp.where(tp == 0, total, foreign)
        high = pltpu.roll(jnp.where(tp == 0, foreign, total), 2, 1)
        total = jnp.where(line < 10, total, jnp.where(line < 12, low, high))
        done_ref[...] = total
        third = []
        for step in range(1, ctx_count):
            third.append(
                pltpu.make_async_remote_copy(
                    done_ref, all_ref.at[ctx], send_three.at[step], recv_three.at[step],
                    device_id={"ctx": peer(step)}, device_id_type=MESH,
                )
            )
            third[-1].start()
        all_ref[ctx] = total
        width = blocks * LANES
        for at in range(part_ref.shape[0] // owners):
            head_copy(at).wait_recv()
            spot = lax.rem(at + lax.rem(ctx + 1, ctx_count) // owners, part_ref.shape[0] // owners)
            rows = next_ref[at]
            after_ref[:, pl.ds(pl.multiple_of(spot * width, LANES), width)] = jnp.where(
                ctx < ctx_count - 1, rows, jnp.zeros_like(rows)
            )
        for copy in third:
            copy.wait_recv()
        out_ref[...] = all_ref[...]
        for step in range(1, ctx_count):
            first_copy(peer(step), ctx).wait_send()
        for at in range(part_ref.shape[0] // owners):
            head_copy(at).wait_send()
        for copy in second + third:
            copy.wait_send()


def finish_kernel(
    blocks, grad_ref, mixed_ref, after_ref, last_ref, weight_ref, sum_ref, grad_out, mixed_out, short_out,
    skip_out,
):
    mixed_out[...] = mixed_ref[...]
    size = grad_ref.shape[1]
    for part in range(3):
        weight = weight_ref[part]
        after = after_ref[2 * part : 2 * part + 2]
        late = last_ref[2 * part : 2 * part + 1] + after[0:1] * weight[2:3]
        final = last_ref[2 * part + 1 : 2 * part + 2] + after[0:1] * weight[1:2] + after[1:2] * weight[2:3]
        grad_out[part, : size - 16] = grad_ref[part, : size - 16]
        tile = grad_ref[part, size - 16 :].astype(jnp.float32)
        row = iota(tile.shape, 0)
        tile = jnp.where(row == 14, late, jnp.where(row == 15, final, tile))
        grad_out[part, size - 16 :] = tile.astype(jnp.bfloat16)
    for block in range(blocks):
        lanes = pl.ds(block * LANES, LANES)
        for part in range(3):
            short_out[part, :, lanes] = sum_ref[block, 3 * part : 3 * part + 3]
        skip_out[:, lanes] = sum_ref[block, 9:10]


def local(projected, upstream, short_weight, skip_gain, residues, rates):
    size = projected.shape[1]
    width = projected.shape[3]
    dp_count, ctx_count, tp_count = (lax.axis_size(name) for name in ("dp", "ctx", "tp"))
    block_count = width // LANES
    own_blocks = block_count // ctx_count
    group_count = width // GROUP
    blocks = math.gcd(block_count, 4)
    wide_blocks = math.gcd(block_count, 8)
    norm = 1.0 / math.sqrt(dp_count * ctx_count * size)

    proj = projected[0].transpose(1, 0, 2)
    up = upstream[0]
    before = shifted(proj[:, size - 2 :], "ctx", 1)
    tp = lax.axis_index("tp")
    ctx = lax.axis_index("ctx")
    my_rates = lax.dynamic_slice_in_dim(rates, tp * group_count, group_count, 0)
    my_residues = lax.dynamic_slice_in_dim(residues, tp * group_count, group_count, 0)
    rate_rows = my_rates.reshape(block_count, 1, LANES)
    gain_rows = (my_residues * jnp.sqrt(my_rates)).reshape(block_count, 1, LANES)
    own_rates = lax.dynamic_slice_in_dim(rate_rows, ctx * own_blocks, own_blocks, 0)
    skip_row = skip_gain.reshape(1, width)

    grid = (block_count // blocks,)
    step_width = blocks * LANES
    wide3 = pl.BlockSpec((3, size, step_width), lambda i: (0, 0, i))
    halo3 = pl.BlockSpec((3, 2, step_width), lambda i: (0, 0, i))
    taps3 = pl.BlockSpec((3, 3, step_width), lambda i: (0, 0, i))
    flat = pl.BlockSpec((size, step_width), lambda i: (0, i))
    line = pl.BlockSpec((1, step_width), lambda i: (0, i))

    def stacked(rows, cols):
        return pl.BlockSpec((blocks, rows, cols), lambda i: (i, 0, 0))

    def array(*shape, kind=jnp.float32):
        return jax.ShapeDtypeStruct(shape, kind)

    row_spec = stacked(1, LANES)
    params = pltpu.CompilerParams(dimension_semantics=("arbitrary",))

    x, states, slopes = pl.pallas_call(
        functools.partial(gather_kernel, blocks),
        grid=grid,
        in_specs=[wide3, halo3, flat, taps3, row_spec],
        out_specs=[stacked(size, 2 * LANES), stacked(GROUP, 2 * LANES), stacked(GROUP, 2 * LANES)],
        out_shape=[
            array(block_count, size, 2 * LANES, kind=jnp.bfloat16),
            array(block_count, GROUP, 2 * LANES),
            array(block_count, GROUP, 2 * LANES),
        ],
        scratch_shapes=[pltpu.VMEM((blocks, 3, size + 8, LANES), jnp.float32)],
        compiler_params=params,
        name="states",
    )(proj, before, up, short_weight, rate_rows)

    vmem = pl.BlockSpec(memory_space=pltpu.VMEM)
    table = (ctx_count, own_blocks, GROUP, 2 * LANES)
    y, modes, carry, extra = pl.pallas_call(
        functools.partial(exchange_kernel, ctx_count, wide_blocks, block_count // wide_blocks // 2),
        in_specs=[vmem] * 5,
        out_specs=[vmem] * 4,
        out_shape=[
            array(block_count, size, 2 * LANES),
            array(block_count, 8, LANES),
            array(*table),
            array(own_blocks, ROWS, LANES),
        ],
        scratch_shapes=[
            pltpu.VMEM(table, jnp.float32),
            pltpu.VMEM(table, jnp.float32),
            pltpu.SemaphoreType.DMA((ctx_count,)),
            pltpu.SemaphoreType.DMA((ctx_count,)),
            pltpu.SemaphoreType.DMA((ctx_count,)),
            pltpu.SemaphoreType.DMA((ctx_count,)),
        ],
        compiler_params=pltpu.CompilerParams(collective_id=1, has_side_effects=True),
        name="exchange",
    )(states.reshape(table), x, rate_rows, gain_rows, own_rates)
    carry = carry.reshape(block_count, GROUP, 2 * LANES)

    owners = blocks // own_blocks
    rounds = block_count // blocks
    others = max(dp_count * tp_count - 1, 1)
    own = (own_blocks, ROWS, LANES)

    def turned(rank, at):
        def index_map(i):
            spot = lax.rem(i + lax.axis_index("ctx") // owners, rounds)
            return tuple(spot if d == at else 0 for d in range(rank))

        return index_map

    def lane_spec(*shape):
        return pl.BlockSpec(shape + (step_width,), turned(len(shape) + 1, len(shape)))

    def block_spec(rows, cols):
        return pl.BlockSpec((blocks, rows, cols), turned(3, 0))

    def whole(*shape):
        return pl.BlockSpec(shape, lambda i: (0,) * len(shape))

    mixed, grad, after, last, summed = pl.pallas_call(
        functools.partial(outer_kernel, (dp_count, ctx_count, tp_count), blocks, norm),
        grid=grid,
        in_specs=[
            lane_spec(3, size), lane_spec(3, 2), lane_spec(size), lane_spec(3, 3), lane_spec(1),
            block_spec(1, LANES), block_spec(1, LANES), block_spec(size, 2 * LANES),
            block_spec(GROUP, 2 * LANES), block_spec(GROUP, 2 * LANES), block_spec(8, LANES),
            whole(*own),
        ],
        out_specs=[
            lane_spec(size), lane_spec(3, size), whole(8, width), lane_spec(8), whole(ctx_count, *own)
        ],
        out_shape=[
            array(size, width, kind=jnp.bfloat16),
            array(3, size, width, kind=jnp.bfloat16),
            array(8, width),
            array(8, width),
            array(ctx_count, *own),
        ],
        scratch_shapes=[
            pltpu.VMEM((blocks, 3, size + 8, LANES), jnp.float32),
            pltpu.VMEM((blocks, 3, size + 8, LANES), jnp.float32),
            pltpu.VMEM((ctx_count,) + own, jnp.float32),
            pltpu.VMEM((rounds, 8, step_width), jnp.float32),
            pltpu.VMEM((rounds, 8, step_width), jnp.float32),
            pltpu.VMEM((ctx_count,) + own, jnp.float32),
            pltpu.VMEM(own, jnp.float32),
            pltpu.VMEM((others,) + own, jnp.float32),
            pltpu.VMEM(own, jnp.float32),
            pltpu.VMEM((ctx_count,) + own, jnp.float32),
            pltpu.SemaphoreType.DMA((ctx_count,)),
            pltpu.SemaphoreType.DMA((ctx_count,)),
            pltpu.SemaphoreType.DMA((others,)),
            pltpu.SemaphoreType.DMA((others,)),
            pltpu.SemaphoreType.DMA((ctx_count,)),
            pltpu.SemaphoreType.DMA((ctx_count,)),
            pltpu.SemaphoreType.DMA((rounds,)),
            pltpu.SemaphoreType.DMA((rounds,)),
        ],
        compiler_params=pltpu.CompilerParams(
            dimension_semantics=("arbitrary",), collective_id=0, has_side_effects=True
        ),
        name="outer",
    )(proj, before, up, short_weight, skip_row, rate_rows, gain_rows, y, carry, slopes, modes, extra)
    summed = summed.reshape(block_count, ROWS, LANES)

    eight = pl.BlockSpec((8, step_width), lambda i: (0, i))
    grad, mixed, grad_short, grad_skip = pl.pallas_call(
        functools.partial(finish_kernel, blocks),
        grid=grid,
        in_specs=[wide3, flat, eight, eight, taps3, stacked(ROWS, LANES)],
        out_specs=[wide3, flat, taps3, line],
        out_shape=[
            array(3, size, width, kind=jnp.bfloat16),
            array(size, width, kind=jnp.bfloat16),
            array(3, 3, width),
            array(1, width),
        ],
        compiler_params=params,
        name="finish",
    )(grad, mixed, after, last, short_weight, summed)

    modes = summed[:, 10 : 10 + 2 * tp_count].reshape(block_count, tp_count, 2, PER_BLOCK, GROUP)
    sum_plain, sum_weighted = (
        modes[:, :, index].transpose(1, 0, 2, 3).reshape(tp_count * group_count, GROUP) for index in range(2)
    )
    root = jnp.sqrt(rates)
    grad_residues = root * sum_plain * norm
    grad_log_rates = residues * (0.5 * root * sum_plain - rates * root * sum_weighted) * norm
    return (
        mixed[None],
        grad.transpose(1, 0, 2)[None],
        grad_short,
        grad_skip.reshape(width),
        grad_residues,
        grad_log_rates,
    )


def solution(mesh):
    in_specs = (
        P("dp", "ctx", None, "tp"),
        P("dp", "ctx", "tp"),
        P(None, None, "tp"),
        P("tp"),
        P(),
        P(),
    )
    out_specs = (
        P("dp", "ctx", "tp"),
        P("dp", "ctx", None, "tp"),
        P(None, None, "tp"),
        P("tp"),
        P(),
        P(),
    )
    return jax.shard_map(local, mesh=mesh, in_specs=in_specs, out_specs=out_specs, check_vma=False)
```
